128 devices in a mesh: gy: 16 (over z_lo, y, core), gx: 8 (over x, z_hi).
Axes of the slice: x: 4, y: 4, z: 4 (z_hi: 2, z_lo: 2; z = z_hi * 2 + z_lo), core: 2. Of those that a mesh axis runs over, the one named last changes fastest.
Arguments:
- frames: bfloat16 [768, 512, 512], P('gy', 'gx'), may hold values from -2.390625 to 2.390625
- hidden_state: bfloat16 [768, 512, 128], P('gy', 'gx'), may hold values from -0.8984375 to 0.8984375
- cell_state: float32 [768, 512, 128], P('gy', 'gx'), may hold values from -4 to 4
- w_gates: bfloat16 [3, 3, 384, 512], replicated, may hold values from -0.3125 to 0.3125
- gate_bias: float32 [512], replicated, may hold values from -3 to 3
- w_qkv: bfloat16 [128, 768], replicated, may hold values from -0.5 to 0.5
- w_out: bfloat16 [256, 128], replicated, may hold values from -0.375 to 0.375
- w_up: bfloat16 [128, 512], replicated, may hold values from -0.5 to 0.5
- w_down: bfloat16 [512, 128], replicated, may hold values from -0.25 to 0.25
Outputs:
- block_out: bfloat16 [768, 512, 128], P('gy', 'gx')
- cell_out: float32 [768, 512, 128], P('gy', 'gx')
The draws below stay inside these ranges and needn't reach their ends.
All inputs are finite; a program needn't handle non-finite values.
Results may differ from the reference program's by a relative error of at most 0.014.
Values may be sent and summed in bfloat16 or wider, within the bound.
A program may use at most 192 MiB of HBM per device.

```python
import jax
import jax.numpy as jnp
from jax import lax

LAT = 256
HID = 128
HEADS = 8
HDIM = 32
MLPW = 512
GRID = 8
ROWS = 768
COLS = 512
EMBED = 256


def shard_levels(rng, shape, shards, least, largest):
    level = 1.0
    for position, shards_of in shards:
        draws = jax.random.uniform(jax.random.fold_in(jax.random.fold_in(rng, 6), position), (shards_of,), jnp.float32, least / len(shards), largest / len(shards))
        level = level * jnp.repeat(jnp.exp(draws), shape[position] // shards_of).reshape((-1,) + (1,) * (len(shape) - 1 - position))
    return level


def centred(rng, extent, scale, limit, split=(), held_as=jnp.bfloat16):
    gain = shard_levels(rng, extent, split, -0.22, 0.18) if split else 1.0
    drawn = jax.random.normal(rng, extent, jnp.float32) * scale * gain
    return jnp.minimum(jnp.maximum(drawn, -limit), limit).astype(held_as)


def setup_inputs(seed: int = 0) -> dict:
    key_of = jax.random.split(jax.random.key(seed), 10)
    return {
        "frames": centred(key_of[0], (ROWS, COLS, 2 * LAT), 0.3, 2.390625, ((0, 16), (1, 8))),
        "hidden_state": jnp.clip(jax.random.uniform(key_of[1], (ROWS, COLS, HID), jnp.float32, -0.8984375, 0.8984375) * shard_levels(key_of[1], (ROWS, COLS, HID), ((0, 16), (1, 8)), -0.4, 0.0), -0.8984375, 0.8984375).astype(jnp.bfloat16),
        "cell_state": centred(key_of[2], (ROWS, COLS, HID), 1.0, 4.0, ((0, 16), (1, 8)), jnp.float32),
        "w_gates": centred(key_of[3], (3, 3, LAT + HID, 4 * HID), (LAT + HID) ** -0.5, 0.3125),
        "gate_bias": centred(key_of[4], (4 * HID,), 0.5, 3.0, (), jnp.float32),
        "w_qkv": centred(key_of[5], (HID, 3 * EMBED), HID ** -0.5, 0.5),
        "w_out": centred(key_of[6], (EMBED, HID), EMBED ** -0.5, 0.375),
        "w_up": centred(key_of[7], (HID, MLPW), HID ** -0.5, 0.5),
        "w_down": centred(key_of[8], (MLPW, HID), MLPW ** -0.5, 0.25),
    }


def layer_norm(values):
    center = values - lax.optimization_barrier(jnp.mean(values, axis=-1, keepdims=True))
    spread = lax.optimization_barrier(jnp.mean(center * center, axis=-1, keepdims=True))
    return center * lax.rsqrt(spread + 1e-05)

def conv_gates(joined, w_gates, gate_bias, out_rows, out_cols):
    channels = joined.shape[2]
    total = jnp.zeros((out_rows * out_cols, w_gates.shape[3]), jnp.float32)
    for row_off in range(3):
        for col_off in range(3):
            window = joined[row_off:row_off + out_rows, col_off:col_off + out_cols].reshape(-1, channels)
            total = total + jnp.dot(window, w_gates[row_off, col_off], preferred_element_type=jnp.float32)
    return total + gate_bias

def lstm_cell(gate_sums, cell_prev):
    width = cell_prev.shape[1]
    in_gate = jax.nn.sigmoid(gate_sums[:, 0:width])
    forget_gate = jax.nn.sigmoid(gate_sums[:, width:2 * width])
    candidate = jnp.tanh(gate_sums[:, 2 * width:3 * width])
    out_gate = jax.nn.sigmoid(gate_sums[:, 3 * width:4 * width])
    new_cell = forget_gate * cell_prev + in_gate * candidate
    new_hidden = (out_gate * jnp.tanh(new_cell)).astype(jnp.bfloat16)
    return (new_cell, new_hidden)

def attend(tokens, w_qkv):
    group_count, length, feature = tokens.shape
    mixed_qkv = jnp.dot(tokens.reshape(-1, feature), w_qkv, preferred_element_type=jnp.float32).astype(jnp.bfloat16)
    mixed_qkv = mixed_qkv.reshape(group_count, length, 3, HEADS, HDIM).astype(jnp.float32)
    queries = mixed_qkv[:, :, 0]
    key_rows = mixed_qkv[:, :, 1]
    values = mixed_qkv[:, :, 2]
    scores = jnp.einsum('gqhd,gkhd->ghqk', queries, key_rows) * HDIM ** (-0.5)
    raised = jnp.exp(scores)
    weights = (raised / lax.optimization_barrier(jnp.sum(raised, axis=-1, keepdims=True))).astype(jnp.bfloat16)
    head_out = jnp.einsum('ghqk,gkhd->gqhd', weights.astype(jnp.float32), values).astype(jnp.bfloat16)
    return head_out.reshape(group_count, length, HEADS * HDIM)

def reference(frames, hidden_state, cell_state, w_gates, gate_bias, w_qkv, w_out, w_up, w_down):
    total_rows, total_cols, width = hidden_state.shape
    latent = frames.shape[2] // 2
    first_in = jnp.pad(jnp.concatenate([frames[:, :, :latent], hidden_state], axis=2), ((1, 1), (1, 1), (0, 0)))
    cell_one, hidden_one = lstm_cell(conv_gates(first_in, w_gates, gate_bias, total_rows, total_cols), cell_state.reshape(-1, width))
    second_in = jnp.concatenate([frames[:, :, latent:], hidden_one.reshape(total_rows, total_cols, width)], axis=2)
    second_in = jnp.pad(second_in, ((1, 1), (1, 1), (0, 0)))
    cell_two, hidden_two = lstm_cell(conv_gates(second_in, w_gates, gate_bias, total_rows, total_cols), cell_one)
    normed = layer_norm(hidden_two.astype(jnp.float32)).astype(jnp.bfloat16)
    stride_y = total_rows // GRID
    stride_x = total_cols // GRID
    grouped = normed.reshape(GRID, stride_y, GRID, stride_x, width).transpose(1, 3, 0, 2, 4)
    grouped = grouped.reshape(stride_y, stride_x, GRID * GRID, width)
    head_out = lax.map(lambda block: attend(block, w_qkv), grouped)
    embed = head_out.shape[-1]
    attended = jnp.dot(head_out.reshape(-1, embed), w_out, preferred_element_type=jnp.float32).astype(jnp.bfloat16)
    attended = attended.reshape(stride_y, stride_x, GRID, GRID, width).transpose(2, 0, 3, 1, 4).reshape(-1, width)
    mixed = hidden_two.astype(jnp.float32) + attended.astype(jnp.float32)
    normed_two = layer_norm(mixed).astype(jnp.bfloat16)
    expanded = jax.nn.gelu(jnp.dot(normed_two, w_up, preferred_element_type=jnp.float32), approximate=True).astype(jnp.bfloat16)
    block_out = (mixed + jnp.dot(expanded, w_down, preferred_element_type=jnp.float32)).astype(jnp.bfloat16)
    return (block_out.reshape(total_rows, total_cols, width), cell_two.reshape(total_rows, total_cols, width))
```

```python
import functools

import jax
import jax.numpy as jnp
from jax import lax
from jax.experimental import pallas as pl
from jax.experimental.pallas import tpu as pltpu
from jax.sharding import PartitionSpec as P

HEADS = 8
HDIM = 32
GRID = 8
SEG = 16
MESH = pl.DeviceIdType.MESH
BF = jnp.bfloat16
F32 = jnp.float32


def sigmoid(t):
    return 0.5 * jnp.tanh(0.5 * t) + 0.5


def layer_norm(values):
    center = values - jnp.mean(values, axis=-1, keepdims=True)
    spread = jnp.mean(center * center, axis=-1, keepdims=True)
    return center * lax.rsqrt(spread + 1e-05)


def fill_row(a_ref, row, cells, left, right, lane):
    count, width = cells.shape
    wide = cells.astype(F32)
    pos = lax.broadcasted_iota(jnp.int32, (count, width), 0)
    before = jnp.where(pos == 0, left, pltpu.roll(wide, 1, 0))
    after = jnp.where(pos == count - 1, right, pltpu.roll(wide, count - 1, 0))
    a_ref[row, :, lane : lane + width] = before.astype(BF)
    a_ref[row, :, lane + width : lane + 2 * width] = cells
    a_ref[row, :, lane + 2 * width : lane + 3 * width] = after.astype(BF)


def gates_of(a_ref, w_ref, bias, row, rows):
    cols, depth = a_ref.shape[1:]
    taps = [a_ref[pl.ds(row + a, rows)].reshape(rows * cols, depth) for a in range(3)]
    return jnp.dot(jnp.concatenate(taps, axis=1), w_ref[...], preferred_element_type=F32) + bias


def lstm(gates, cell):
    width = cell.shape[1]
    new_cell = sigmoid(gates[:, width : 2 * width]) * cell + sigmoid(gates[:, :width]) * jnp.tanh(
        gates[:, 2 * width : 3 * width]
    )
    return new_cell, sigmoid(gates[:, 3 * width :]) * jnp.tanh(new_cell)


def conv_kernel(norm, f_ref, h_ref, rowf, rowh, colf, colh, cell_ref, w_ref, b_ref, *rest):
    if norm:
        hid_ref, cell_out, normed_ref, a_ref = rest
    else:
        hid_ref, cell_out, a_ref = rest
    rows, cols, width = h_ref.shape
    for c_ref, r_ref, k_ref, lane in ((f_ref, rowf, colf, 0), (h_ref, rowh, colh, 3 * f_ref.shape[2])):

        def put(row, cells):
            fill_row(a_ref, row, cells, k_ref[0, pl.ds(row, 1), :], k_ref[1, pl.ds(row, 1), :], lane)

        put(0, r_ref[0])
        put(rows + 1, r_ref[1])

        def fill(r, _):
            put(r + 1, c_ref[r])
            return 0

        lax.fori_loop(0, rows, fill, 0)
    bias = b_ref[...]
    step = 8

    def chunk(i, _):
        row = i * step
        gates = gates_of(a_ref, w_ref, bias, row, step)
        new_cell, hid = lstm(gates, cell_ref[pl.ds(row, step)].reshape(step * cols, width))
        hid = hid.astype(BF)
        cell_out[pl.ds(row, step)] = new_cell.reshape(step, cols, width)
        hid_ref[pl.ds(row, step)] = hid.reshape(step, cols, width)
        if norm:
            normed_ref[pl.ds(row, step)] = layer_norm(hid.astype(F32)).astype(BF).reshape(step, cols, width)
        return 0

    lax.fori_loop(0, rows // step, chunk, 0)


def vmem(count):
    return [pl.BlockSpec(memory_space=pltpu.VMEM)] * count


def params(**more):
    return pltpu.CompilerParams(vmem_limit_bytes=60 * 2**20, **more)


def conv(norm, frame, hidden, rowf, rowh, colf, colh, cell, weights, bias):
    rows, cols, width = hidden.shape
    depth = 3 * (frame.shape[2] + width)
    outs = [jax.ShapeDtypeStruct(hidden.shape, BF), jax.ShapeDtypeStruct(hidden.shape, F32)]
    if norm:
        outs.append(jax.ShapeDtypeStruct(hidden.shape, BF))
    return pl.pallas_call(
        functools.partial(conv_kernel, norm),
        out_shape=outs,
        in_specs=vmem(9),
        out_specs=vmem(len(outs)),
        scratch_shapes=[pltpu.VMEM((rows + 2, cols, depth), BF)],
        compiler_params=params(),
        name=f"conv{int(norm)}",
    )(frame, hidden, rowf, rowh, colf, colh, cell, weights, bias)


def peer(j, parity):
    return {"gy": 2 * (j // 8) + parity, "gx": j % 8}


def exchange_kernel(src, dst, send_sem, recv_sem, own_sem):
    gy, gx = lax.axis_index("gy"), lax.axis_index("gx")
    parity = gy % 2
    me = (gy // 2) * 8 + gx
    count = src.shape[0]
    barrier = pltpu.get_barrier_semaphore()

    def greet(i, _):
        j = (me + i) % count
        pl.semaphore_signal(barrier, inc=1, device_id=peer(j, parity), device_id_type=MESH)
        return 0

    lax.fori_loop(1, count, greet, 0)
    own = pltpu.make_async_copy(src.at[me], dst.at[me], own_sem)
    own.start()
    pl.semaphore_wait(barrier, count - 1)

    def send(i, _):
        j = (me + i) % count
        pltpu.make_async_remote_copy(
            src_ref=src.at[j],
            dst_ref=dst.at[me],
            send_sem=send_sem,
            recv_sem=recv_sem,
            device_id=peer(j, parity),
            device_id_type=MESH,
        ).start()
        return 0

    lax.fori_loop(1, count, send, 0)
    own.wait()
    rest = pltpu.make_async_remote_copy(
        src_ref=src.at[pl.ds(0, count - 1)],
        dst_ref=dst.at[pl.ds(0, count - 1)],
        send_sem=send_sem,
        recv_sem=recv_sem,
        device_id=peer(me, parity),
        device_id_type=MESH,
    )
    rest.wait_send()
    rest.wait_recv()


def exchange(parts, number):
    return pl.pallas_call(
        exchange_kernel,
        out_shape=jax.ShapeDtypeStruct(parts.shape, parts.dtype),
        in_specs=[pl.BlockSpec(memory_space=pl.ANY)],
        out_specs=pl.BlockSpec(memory_space=pl.ANY),
        scratch_shapes=[pltpu.SemaphoreType.DMA, pltpu.SemaphoreType.DMA, pltpu.SemaphoreType.DMA],
        compiler_params=pltpu.CompilerParams(collective_id=number, has_side_effects=True),
        name=f"exchange{number}",
    )(parts)


def head_mask():
    row = lax.broadcasted_iota(jnp.int32, (256, 256), 0)
    col = lax.broadcasted_iota(jnp.int32, (256, 256), 1)
    heads = ((col % 128) // HDIM == row // 64).astype(F32).astype(BF)
    blocks = (col // 64 == row // 64).astype(F32).astype(BF)
    return heads, blocks


def attend_chunk(tokens, w_qkv, w_out, heads, blocks, wide, qkv, prob, outs):
    members = tokens.shape[0]
    cells = members * SEG
    wide[...] = tokens.reshape(cells, 128).astype(F32)
    grouped = jnp.concatenate([wide[pl.ds(g, members, stride=SEG), :] for g in range(SEG)], axis=0).astype(BF)
    qkv[...] = jnp.dot(grouped, w_qkv[...], preferred_element_type=F32).astype(BF)
    zero = jnp.zeros((64, 128), BF)

    def spread(base, lane):
        pair = jnp.concatenate(
            [qkv[pl.ds(base, 64), lane : lane + 128], qkv[pl.ds(base + 64, 64), lane : lane + 128]], axis=1
        )
        return jnp.concatenate([pair] * 4, axis=0) * heads

    def score(p, _):
        base = pl.multiple_of(p * 128, 128)
        for half in range(2):
            lane = half * 128
            q1 = jnp.concatenate([qkv[pl.ds(base, 64), lane : lane + 128], zero], axis=1)
            q2 = jnp.concatenate([zero, qkv[pl.ds(base + 64, 64), lane : lane + 128]], axis=1)
            s = lax.dot_general(
                jnp.concatenate([q1, q2], axis=0),
                spread(base, 256 + lane),
                (((1,), (1,)), ((), ())),
                preferred_element_type=F32,
            )
            raised = jnp.minimum(jnp.exp(s * HDIM**-0.5), 3.3895e38).astype(BF)
            prob[half, pl.ds(base, 128), :] = raised
        return 0

    lax.fori_loop(0, SEG // 2, score, 0)
    step = 256

    def share(i, _):
        base = pl.multiple_of(i * step, step)
        for half in range(2):
            raised = prob[half, pl.ds(base, step), :]
            total = jnp.dot(raised, blocks, preferred_element_type=F32)
            prob[half, pl.ds(base, step), :] = (raised.astype(F32) / total).astype(BF)
        return 0

    lax.fori_loop(0, cells // step, share, 0)

    def gather(p, _):
        base = pl.multiple_of(p * 128, 128)
        for half in range(2):
            lane = half * 128
            o = jnp.dot(prob[half, pl.ds(base, 128), :], spread(base, 512 + lane), preferred_element_type=F32)
            outs[pl.ds(base, 64), lane : lane + 128] = o[:64, :128].astype(BF)
            outs[pl.ds(base + 64, 64), lane : lane + 128] = o[64:, 128:].astype(BF)
        return 0

    lax.fori_loop(0, SEG // 2, gather, 0)
    wide[...] = jnp.dot(outs[...], w_out[...], preferred_element_type=F32)


def attend_kernel(tok_ref, w_qkv, w_out, out_ref, wide, qkv, prob, outs):
    heads, blocks = head_mask()
    members = tok_ref.shape[0]
    for c in range(tok_ref.shape[1]):
        attend_chunk(tok_ref[:, c], w_qkv, w_out, heads, blocks, wide, qkv, prob, outs)

        def ungroup(m, _):
            out_ref[m, c] = wide[pl.ds(m, SEG, stride=members), :].astype(BF)
            return 0

        lax.fori_loop(0, members, ungroup, 0, unroll=8)


def attend(tokens, w_qkv, w_out):
    cells = tokens.shape[0] * SEG
    return pl.pallas_call(
        attend_kernel,
        out_shape=jax.ShapeDtypeStruct(tokens.shape, BF),
        in_specs=vmem(3),
        out_specs=vmem(1)[0],
        scratch_shapes=[
            pltpu.VMEM((cells, 128), F32),
            pltpu.VMEM((cells, 768), BF),
            pltpu.VMEM((2, cells, 256), BF),
            pltpu.VMEM((cells, 256), BF),
        ],
        compiler_params=params(),
        name="attend",
    )(tokens, w_qkv, w_out)


def mlp_rows(hidden, attended, w_up, w_down):
    mixed = hidden.astype(F32) + attended.astype(F32)
    normed = layer_norm(mixed).astype(BF)
    u = jnp.dot(normed, w_up[...], preferred_element_type=F32)
    expanded = (0.5 * u * (1.0 + jnp.tanh(0.7978845608 * (u + 0.044715 * (u * u * u))))).astype(BF)
    return (mixed + jnp.dot(expanded, w_down[...], preferred_element_type=F32)).astype(BF)


def mlp_kernel(hid_ref, att_ref, w_up, w_down, out_ref):
    step = 512

    def chunk(i, _):
        at = pl.ds(pl.multiple_of(i * step, step), step)
        out_ref[at, :] = mlp_rows(hid_ref[at, :], att_ref[at, :], w_up, w_down)
        return 0

    lax.fori_loop(0, hid_ref.shape[0] // step, chunk, 0)


def mlp(hidden, attended, w_up, w_down):
    return pl.pallas_call(
        mlp_kernel,
        out_shape=jax.ShapeDtypeStruct(hidden.shape, BF),
        in_specs=vmem(4),
        out_specs=vmem(1)[0],
        compiler_params=params(),
        name="mlp",
    )(hidden, attended, w_up, w_down)


def halos(cells):
    def both(low, high, axis):
        count = lax.axis_size(axis)
        return (
            lax.ppermute(high, axis, [(i, i + 1) for i in range(count - 1)]),
            lax.ppermute(low, axis, [(i + 1, i) for i in range(count - 1)]),
        )

    rows = cells.shape[0]
    up, down = both(cells[0], cells[-1], "gy")

    def side(at):
        return jnp.concatenate([up[at][None], cells[:, at], down[at][None]], axis=0)

    left, right = both(side(0), side(-1), "gx")
    cols = jnp.pad(jnp.stack([left, right]), ((0, 0), (0, 6), (0, 0)))
    return jnp.stack([up, down]), cols.astype(F32)


def body(frames, hidden_state, cell_state, w_gates, gate_bias, w_qkv, w_out, w_up, w_down):
    rows, cols, width = hidden_state.shape
    latent = frames.shape[2] // 2
    first, second = frames[:, :, :latent], frames[:, :, latent:]
    stacked = jnp.concatenate([first, hidden_state, second], axis=2)
    row_in, col_in = halos(stacked)
    weights = jnp.concatenate(
        [
            w_gates[:, :, :latent].reshape(3, 3 * latent, -1),
            w_gates[:, :, latent:].reshape(3, 3 * width, -1),
        ],
        axis=1,
    ).reshape(-1, w_gates.shape[3])
    bias = gate_bias[None]
    a, b = latent, latent + width
    hid_one, cell_one = conv(
        False, first, hidden_state, row_in[..., :a], row_in[..., a:b], col_in[..., :a], col_in[..., a:b],
        cell_state, weights, bias,
    )
    row_one, col_one = halos(hid_one)
    hid_two, cell_two, normed = conv(
        True, second, hid_one, row_in[..., b:], row_one, col_in[..., b:], col_one, cell_one, weights, bias
    )
    parts = normed.reshape(rows // SEG, 64, SEG, width).transpose(1, 0, 2, 3)
    tokens = exchange(parts, 1)
    landed = exchange(attend(tokens, w_qkv, w_out), 2)
    attended = landed.transpose(1, 0, 2, 3).reshape(rows * cols, width)
    block = mlp(hid_two.reshape(rows * cols, width), attended, w_up, w_down)
    return block.reshape(rows, cols, width), cell_two


def solution(mesh):
    spec = P("gy", "gx", None)
    return jax.shard_map(
        body,
        mesh=mesh,
        in_specs=(spec, spec, spec, P(), P(), P(), P(), P(), P()),
        out_specs=(spec, spec),
        check_vma=False,
    )
```

```python
import jax
import jax.numpy as jnp
from jax import lax
from jax.experimental import pallas as pl
from jax.experimental.pallas import tpu as pltpu
from jax.sharding import PartitionSpec as P

HEADS = 8
HDIM = 32
GRID = 8
SEG = 16
PITCH = 72
MESH = pl.DeviceIdType.MESH
BF = jnp.bfloat16
F32 = jnp.float32


def sigmoid(t):
    return 0.5 * jnp.tanh(0.5 * t) + 0.5


def layer_norm(values):
    center = values - jnp.mean(values, axis=-1, keepdims=True)
    spread = jnp.mean(center * center, axis=-1, keepdims=True)
    return center * lax.rsqrt(spread + 1e-05)


def shifted_row(a_ref, row, cells, lane):
    count, width = cells.shape
    wide = cells.astype(F32)
    a_ref[row, :, lane : lane + width] = pltpu.roll(wide, 1, 0).astype(BF)
    a_ref[row, :, lane + width : lane + 2 * width] = cells
    a_ref[row, :, lane + 2 * width : lane + 3 * width] = pltpu.roll(wide, count - 1, 0).astype(BF)


def patch_row(a_ref, row, left, right, lane):
    cols, width = a_ref.shape[1], left.shape[1]
    pos = lax.broadcasted_iota(jnp.int32, (SEG, width), 0)
    tile = a_ref[row, 0:SEG, lane : lane + width].astype(F32)
    a_ref[row, 0:SEG, lane : lane + width] = jnp.where(pos == 0, left, tile).astype(BF)
    lane += 2 * width
    tile = a_ref[row, cols - SEG : cols, lane : lane + width].astype(F32)
    a_ref[row, cols - SEG : cols, lane : lane + width] = jnp.where(pos == SEG - 1, right, tile).astype(BF)


def gates_of(a_ref, w_ref, bias, row, rows, col, cols):
    depth = a_ref.shape[2]
    taps = [a_ref[pl.ds(row + a, rows), col : col + cols, :].reshape(rows * cols, depth) for a in range(3)]
    return jnp.dot(jnp.concatenate(taps, axis=1), w_ref[...], preferred_element_type=F32) + bias


def lstm(gates, cell):
    width = cell.shape[1]
    new_cell = sigmoid(gates[:, width : 2 * width]) * cell + sigmoid(gates[:, :width]) * jnp.tanh(
        gates[:, 2 * width : 3 * width]
    )
    return new_cell, sigmoid(gates[:, 3 * width :]) * jnp.tanh(new_cell)


def peer(j, parity, columns):
    return {"gy": 2 * (j // columns) + parity, "gx": j % columns}


class Shift:
    def __init__(self, src, dst, dy, dx, send_sem, recv_sem):
        gy, gx = lax.axis_index("gy"), lax.axis_index("gx")
        ny, nx = lax.axis_size("gy"), lax.axis_size("gx")

        def inside(y, x):
            return jnp.logical_and(jnp.logical_and(y >= 0, y < ny), jnp.logical_and(x >= 0, x < nx))

        self.dst = dst
        self.to = inside(gy + dy, gx + dx)
        self.come = inside(gy - dy, gx - dx)
        self.copy = pltpu.make_async_remote_copy(
            src_ref=src,
            dst_ref=dst,
            send_sem=send_sem,
            recv_sem=recv_sem,
            device_id={"gy": gy + dy, "gx": gx + dx},
            device_id_type=MESH,
        )

    def clear(self):
        @pl.when(jnp.logical_not(self.come))
        def _():
            self.dst[...] = jnp.zeros(self.dst.shape, self.dst.dtype)

    def start(self):
        @pl.when(self.to)
        def _():
            self.copy.start()

    def wait_recv(self):
        @pl.when(self.come)
        def _():
            self.copy.wait_recv()

    def wait_send(self):
        @pl.when(self.to)
        def _():
            self.copy.wait_send()


def shifts(pieces, cols_out, cols_in, send_sems, recv_sems):
    plan = []

    def add(src, dst, dy, dx):
        at = len(plan)
        plan.append(Shift(src, dst, dy, dx, send_sems.at[at], recv_sems.at[at]))

    for side, dx in ((1, -1), (0, 1)):
        add(cols_out.at[1 - side], cols_in.at[side], 0, dx)
    for cells, rows_in, corners in pieces:
        rows, cols = cells.shape[:2]
        add(cells.at[0], rows_in.at[1], -1, 0)
        add(cells.at[rows - 1], rows_in.at[0], 1, 0)
        for dy, row, low in ((-1, 0, 2), (1, rows - 1, 0)):
            add(cells.at[row, pl.ds(0, SEG)], corners.at[low + 1], dy, -1)
            add(cells.at[row, pl.ds(cols - SEG, SEG)], corners.at[low], dy, 1)
    return plan


def edge_columns(cells, cols_out, scratch, lane):
    rows, cols, width = cells.shape

    def eight(i, _):
        base = pl.multiple_of(i * 8, 8)
        low = [cells[base + k, 0:SEG, :].astype(F32)[0:1] for k in range(8)]
        high = [cells[base + k, cols - SEG : cols, :].astype(F32)[SEG - 1 : SEG] for k in range(8)]
        scratch[0, pl.ds(base, 8), lane : lane + width] = jnp.concatenate(low, axis=0)
        scratch[1, pl.ds(base, 8), lane : lane + width] = jnp.concatenate(high, axis=0)
        return 0

    lax.fori_loop(0, rows // 8, eight, 0)
    cols_out[:, :, lane : lane + width] = scratch[:, 0:rows, lane : lane + width].astype(BF)


def corner(ref, side, lanes):
    wide = ref[:, lanes].astype(F32)
    return wide[SEG - 1 : SEG] if side == 0 else wide[0:1]

def head_mask():
    row = lax.broadcasted_iota(jnp.int32, (256, 256), 0)
    col = lax.broadcasted_iota(jnp.int32, (256, 256), 1)
    heads = ((col % 128) // HDIM == row // 64).astype(F32).astype(BF)
    blocks = (col // 64 == row // 64).astype(F32).astype(BF)
    return heads, blocks


def attend_chunk(tokens, w_qkv, w_out, heads, blocks, wide, qkv, prob, outs):
    members = tokens.shape[0]
    cells = members * SEG
    wide[0:cells, :] = tokens.reshape(cells, 128).astype(F32)
    grouped = jnp.concatenate([wide[pl.ds(g, members, stride=SEG), :] for g in range(SEG)], axis=0).astype(BF)
    qkv[...] = jnp.dot(grouped, w_qkv[...], preferred_element_type=F32).astype(BF)
    zero = jnp.zeros((64, 128), BF)

    def spread(base, lane):
        pair = jnp.concatenate([qkv[base : base + 64, lane : lane + 128], qkv[base + 64 : base + 128, lane : lane + 128]], axis=1)
        return jnp.concatenate([pair] * 4, axis=0) * heads

    for base in range(0, cells, 128):
        for half in range(2):
            lane = half * 128
            q1 = jnp.concatenate([qkv[base : base + 64, lane : lane + 128], zero], axis=1)
            q2 = jnp.concatenate([zero, qkv[base + 64 : base + 128, lane : lane + 128]], axis=1)
            s = lax.dot_general(
                jnp.concatenate([q1, q2], axis=0),
                spread(base, 256 + lane),
                (((1,), (1,)), ((), ())),
                preferred_element_type=F32,
            )
            prob[half, base : base + 128, :] = jnp.minimum(jnp.exp(s * HDIM**-0.5), 3.3895e38).astype(BF)
    step = 512
    for base in range(0, cells, step):
        for half in range(2):
            raised = prob[half, base : base + step, :]
            total = jnp.dot(raised, blocks, preferred_element_type=F32)
            prob[half, base : base + step, :] = (raised.astype(F32) * (1.0 / total)).astype(BF)
    for base in range(0, cells, 128):
        for half in range(2):
            lane = half * 128
            o = jnp.dot(prob[half, base : base + 128, :], spread(base, 512 + lane), preferred_element_type=F32)
            outs[base : base + 64, lane : lane + 128] = o[:64, :128].astype(BF)
            outs[base + 64 : base + 128, lane : lane + 128] = o[64:, 128:].astype(BF)
    done = jnp.dot(outs[...], w_out[...], preferred_element_type=F32)
    for g in range(SEG):
        wide[g * PITCH : g * PITCH + members, :] = done[g * members : (g + 1) * members]


def mlp_rows(hidden, attended, w_up, w_down):
    mixed = hidden.astype(F32) + attended.astype(F32)
    normed = layer_norm(mixed).astype(BF)
    u = jnp.dot(normed, w_up[...], preferred_element_type=F32)
    twice = u + u * jnp.tanh(u * (0.7978845608 + 0.7978845608 * 0.044715 * (u * u)))
    return (mixed + 0.5 * jnp.dot(twice.astype(BF), w_down[...], preferred_element_type=F32)).astype(BF)


def kernel(*refs):
    names = iter(refs)
    take = lambda n: [next(names) for _ in range(n)]
    frames, hidden, cell, w_gates, bias_in, wqkv_in, wout_in, wup_in, wdown_in = take(9)
    block_out, cell_out = take(2)
    fr, hd, cl, w, bias_v, w_qkv, w_out, w_up, w_down = take(9)
    a1, a2, h1, h2, normed, tok, ret, land, outb = take(9)
    rowf, rowh, cornf, cornh, cols_out, cols_in, edge = take(7)
    row1, corn1, cols_out1, cols_in1 = take(4)
    wide, qkv, prob, outs = take(4)
    load_sem, s_send, s_recv, s_send1, s_recv1, to_send, to_recv, back_send, back_recv, out_sem = take(10)

    rows, cols, width = hd.shape
    latent = fr.shape[2] // 2
    gy, gx = lax.axis_index("gy"), lax.axis_index("gx")
    ny, nx = lax.axis_size("gy"), lax.axis_size("gx")
    parity = gy % 2
    count = ny // 2 * nx
    me = (gy // 2) * nx + gx

    loads = [
        pltpu.make_async_copy(src, dst, load_sem.at[i])
        for i, (src, dst) in enumerate(
            ((frames, fr), (hidden, hd), (cell, cl), (bias_in, bias_v), (wqkv_in, w_qkv), (wout_in, w_out), (wup_in, w_up), (wdown_in, w_down))
        )
    ]
    gate_loads = []
    depth = 3 * (latent + width)
    for a in range(3):
        for b in range(3):
            gate_loads.append((w_gates.at[a, b, pl.ds(0, latent)], w.at[pl.ds(a * depth + b * latent, latent)]))
            gate_loads.append(
                (w_gates.at[a, b, pl.ds(latent, width)], w.at[pl.ds(a * depth + 3 * latent + b * width, width)])
            )
    gate_loads = [pltpu.make_async_copy(s, d, load_sem.at[8 + i]) for i, (s, d) in enumerate(gate_loads)]

    first = shifts(((fr, rowf, cornf), (hd, rowh, cornh)), cols_out, cols_in, s_send, s_recv)
    second = shifts(((h1, row1, corn1),), cols_out1, cols_in1, s_send1, s_recv1)

    loads[0].start()
    loads[1].start()
    barrier = pltpu.get_barrier_semaphore()

    def greet(i, _):
        pl.semaphore_signal(barrier, inc=1, device_id=peer((me + i) % count, parity, nx), device_id_type=MESH)
        return 0

    lax.fori_loop(1, count, greet, 0)
    greeted = count - 1
    for dy in (-1, 1):
        for dx in (-1, 0, 1):
            y, x = gy + dy, gx + dx
            near = jnp.logical_and(jnp.logical_and(y >= 0, y < ny), jnp.logical_and(x >= 0, x < nx))

            @pl.when(near)
            def _():
                pl.semaphore_signal(barrier, inc=1, device_id={"gy": y, "gx": x}, device_id_type=MESH)

            greeted = greeted + near.astype(jnp.int32)
    for copy in gate_loads + loads[2:]:
        copy.start()
    for shift in first + second:
        shift.clear()

    loads[0].wait()
    loads[1].wait()
    edge_columns(fr, cols_out, edge, 0)
    edge_columns(hd, cols_out, edge, 2 * latent)

    def build(r, _):
        shifted_row(a1, r + 1, fr[r, :, 0:latent], 0)
        shifted_row(a1, r + 1, hd[r], 3 * latent)
        shifted_row(a2, r + 1, fr[r, :, latent : 2 * latent], 0)
        return 0

    lax.fori_loop(0, rows, build, 0)
    pl.semaphore_wait(barrier, greeted)
    for shift in first:
        shift.start()

    for copy in gate_loads:
        copy.wait()
    loads[2].wait()
    loads[3].wait()
    bias = bias_v[...]

    def step_one(row, count_r, col, count_c):
        cells = count_r * count_c
        old = cl[pl.ds(row, count_r), col : col + count_c, :].reshape(cells, width)
        new_cell, hid = lstm(gates_of(a1, w, bias, row, count_r, col, count_c), old)
        cl[pl.ds(row, count_r), col : col + count_c, :] = new_cell.reshape(count_r, count_c, width)
        h1[pl.ds(row, count_r), col : col + count_c, :] = hid.astype(BF).reshape(count_r, count_c, width)

    step_one(8, 16, SEG, cols - 2 * SEG)

    for shift in first:
        shift.wait_recv()
    side_in = edge
    side_in[:, 0:rows, :] = cols_in[...].astype(F32)

    def patch(i, _):
        base = pl.multiple_of(i * 8, 8)
        left, right = side_in[0, pl.ds(base, 8), :], side_in[1, pl.ds(base, 8), :]
        for k in range(8):
            lk, rk = left[k : k + 1], right[k : k + 1]
            patch_row(a1, base + k + 1, lk[:, :latent], rk[:, :latent], 0)
            patch_row(a1, base + k + 1, lk[:, 2 * latent :], rk[:, 2 * latent :], 3 * latent)
            patch_row(a2, base + k + 1, lk[:, latent : 2 * latent], rk[:, latent : 2 * latent], 0)
        return 0

    lax.fori_loop(0, rows // 8, patch, 0)
    everything = slice(None)

    def outer(a_ref, rows_in, corners, lanes, lane):
        for end, row in ((0, 0), (1, rows + 1)):
            shifted_row(a_ref, row, rows_in[end, :, lanes], lane)
            patch_row(
                a_ref, row, corner(corners.at[2 * end], 0, lanes), corner(corners.at[2 * end + 1], 1, lanes), lane
            )

    outer(a1, rowf, cornf, slice(0, latent), 0)
    outer(a1, rowh, cornh, everything, 3 * latent)
    outer(a2, rowf, cornf, slice(latent, 2 * latent), 0)

    step_one(0, 8, 0, cols)
    step_one(rows - 8, 8, 0, cols)
    step_one(8, 32, 0, SEG)
    step_one(8, 32, cols - SEG, SEG)
    edge_columns(h1, cols_out1, edge, 0)
    for shift in second:
        shift.start()
    step_one(24, 16, SEG, cols - 2 * SEG)

    def build_two(r, _):
        shifted_row(a2, r + 1, h1[r], 3 * latent)
        return 0

    lax.fori_loop(0, rows, build_two, 0, unroll=2)
    for shift in second:
        shift.wait_recv()
    side_in[:, 0:rows, 0:width] = cols_in1[...].astype(F32)

    def patch_two(i, _):
        base = pl.multiple_of(i * 8, 8)
        left, right = side_in[0, pl.ds(base, 8), 0:width], side_in[1, pl.ds(base, 8), 0:width]
        for k in range(8):
            patch_row(a2, base + k + 1, left[k : k + 1], right[k : k + 1], 3 * latent)
        return 0

    lax.fori_loop(0, rows // 8, patch_two, 0)
    outer(a2, row1, corn1, everything, 3 * latent)

    step = 8
    quarters = cols // SEG
    sent = step * quarters

    def step_two(s, _):
        row = s * step
        cells = step * cols
        new_cell, hid = lstm(
            gates_of(a2, w, bias, row, step, 0, cols), cl[pl.ds(row, step)].reshape(cells, width)
        )
        cl[pl.ds(row, step)] = new_cell.reshape(step, cols, width)
        hid = hid.astype(BF)
        h2[pl.ds(row * quarters, sent)] = hid.reshape(sent, SEG, width)
        normed[pl.ds(row * quarters, sent)] = layer_norm(hid.astype(F32)).astype(BF).reshape(sent, SEG, width)
        pltpu.make_async_copy(cl.at[pl.ds(row, step)], cell_out.at[pl.ds(row, step)], out_sem.at[0]).start()
        c, half = s // 2, s % 2

        def send(t, _):
            j = half * sent + (me + t) % sent

            @pl.when(j != me)
            def _():
                pltpu.make_async_remote_copy(
                    src_ref=normed.at[c * count + j],
                    dst_ref=tok.at[c, me],
                    send_sem=to_send,
                    recv_sem=to_recv.at[c],
                    device_id=peer(j, parity, nx),
                    device_id_type=MESH,
                ).start()

            return 0

        lax.fori_loop(0, sent, send, 0)
        return 0

    lax.fori_loop(0, rows // step, step_two, 0)
    for copy in loads[4:]:
        copy.wait()
    heads, blocks = head_mask()
    chunks = tok.shape[0]

    def attend_step(c, _):
        tok[c, me] = normed[c * count + me]
        arrived = tok.at[c, pl.ds(0, count - 1)]
        pltpu.make_async_remote_copy(
            src_ref=arrived, dst_ref=arrived, send_sem=to_send, recv_sem=to_recv.at[c],
            device_id=peer(me, parity, nx), device_id_type=MESH,
        ).wait_recv()
        attend_chunk(tok[c], w_qkv, w_out, heads, blocks, wide, qkv, prob, outs)
        for m in range(count):
            ret[c, m] = wide[pl.ds(m, SEG, stride=PITCH), :].astype(BF)

        def send(t, _):
            m = (me + t) % count
            pltpu.make_async_remote_copy(
                src_ref=ret.at[c, m],
                dst_ref=land.at[c * count + me],
                send_sem=back_send,
                recv_sem=back_recv.at[c],
                device_id=peer(m, parity, nx),
                device_id_type=MESH,
            ).start()
            return 0

        lax.fori_loop(1, count, send, 0)
        land[c * count + me] = ret[c, me]
        return 0

    lax.fori_loop(0, chunks, attend_step, 0)

    def mlp_step(c, _):
        base = c * count
        arrived = land.at[pl.ds(base, count - 1)]
        pltpu.make_async_remote_copy(
            src_ref=arrived, dst_ref=arrived, send_sem=back_send, recv_sem=back_recv.at[c],
            device_id=peer(me, parity, nx), device_id_type=MESH,
        ).wait_recv()
        cells = count * SEG
        result = mlp_rows(
            h2[pl.ds(base, count)].reshape(cells, width), land[pl.ds(base, count)].reshape(cells, width), w_up, w_down
        )
        outb[pl.ds(c * SEG, SEG)] = result.reshape(SEG, cols, width)
        pltpu.make_async_copy(outb.at[pl.ds(c * SEG, SEG)], block_out.at[pl.ds(c * SEG, SEG)], out_sem.at[1]).start()
        return 0

    lax.fori_loop(0, chunks, mlp_step, 0)
    for shift in first + second:
        shift.wait_send()
    for sem, source in ((to_send, tok), (back_send, ret)):
        most = source.at[:, pl.ds(0, count - 1)]
        pltpu.make_async_remote_copy(
            src_ref=most, dst_ref=most, send_sem=sem, recv_sem=to_recv.at[0],
            device_id=peer(me, parity, nx), device_id_type=MESH,
        ).wait_send()
    pltpu.make_async_copy(cl, cell_out, out_sem.at[0]).wait()
    pltpu.make_async_copy(outb, block_out, out_sem.at[1]).wait()


def body(frames, hidden_state, cell_state, w_gates, gate_bias, w_qkv, w_out, w_up, w_down):
    rows, cols, width = hidden_state.shape
    both = frames.shape[2]
    depth = 3 * (both // 2 + width)
    members = lax.axis_size("gy") // 2 * lax.axis_size("gx")
    chunks = rows * cols // (members * SEG)
    cells = members * SEG
    any_space = pl.BlockSpec(memory_space=pl.ANY)
    dma = pltpu.SemaphoreType.DMA
    scratch = [
        pltpu.VMEM(frames.shape, BF),
        pltpu.VMEM(hidden_state.shape, BF),
        pltpu.VMEM(cell_state.shape, F32),
        pltpu.VMEM((3 * depth, w_gates.shape[3]), BF),
        pltpu.VMEM((1, gate_bias.shape[0]), F32),
        pltpu.VMEM(w_qkv.shape, BF),
        pltpu.VMEM(w_out.shape, BF),
        pltpu.VMEM(w_up.shape, BF),
        pltpu.VMEM(w_down.shape, BF),
        pltpu.VMEM((rows + 2, cols, depth), BF),
        pltpu.VMEM((rows + 2, cols, depth), BF),
        pltpu.VMEM((rows, cols, width), BF),
        pltpu.VMEM((chunks * members, SEG, width), BF),
        pltpu.VMEM((chunks * members, SEG, width), BF),
        pltpu.VMEM((chunks, members, SEG, width), BF),
        pltpu.VMEM((chunks, members, SEG, width), BF),
        pltpu.VMEM((chunks * members, SEG, width), BF),
        pltpu.VMEM((rows, cols, width), BF),
        pltpu.VMEM((2, cols, both), BF),
        pltpu.VMEM((2, cols, width), BF),
        pltpu.VMEM((4, SEG, both), BF),
        pltpu.VMEM((4, SEG, width), BF),
        pltpu.VMEM((2, rows, both + width), BF),
        pltpu.VMEM((2, rows, both + width), BF),
        pltpu.VMEM((2, rows, both + width), F32),
        pltpu.VMEM((2, cols, width), BF),
        pltpu.VMEM((4, SEG, width), BF),
        pltpu.VMEM((2, rows, width), BF),
        pltpu.VMEM((2, rows, width), BF),
        pltpu.VMEM((SEG * PITCH, width), F32),
        pltpu.VMEM((cells, 3 * HEADS * HDIM), BF),
        pltpu.VMEM((2, cells, 256), BF),
        pltpu.VMEM((cells, HEADS * HDIM), BF),
        dma((26,)),
        dma((14,)),
        dma((14,)),
        dma((8,)),
        dma((8,)),
        dma,
        dma((chunks,)),
        dma,
        dma((chunks,)),
        dma((2,)),
    ]
    return pl.pallas_call(
        kernel,
        out_shape=(jax.ShapeDtypeStruct(hidden_state.shape, BF), jax.ShapeDtypeStruct(cell_state.shape, F32)),
        in_specs=[any_space] * 9,
        out_specs=[any_space] * 2,
        scratch_shapes=scratch,
        compiler_params=pltpu.CompilerParams(vmem_limit_bytes=60 * 2**20, collective_id=1, has_side_effects=True),
        name="fused",
    )(frames, hidden_state, cell_state, w_gates, gate_bias[None], w_qkv, w_out, w_up, w_down)


def solution(mesh):
    spec = P("gy", "gx", None)
    return jax.shard_map(
        body,
        mesh=mesh,
        in_specs=(spec, spec, spec, P(), P(), P(), P(), P(), P()),
        out_specs=(spec, spec),
        check_vma=False,
    )
```

```python
import jax
import jax.numpy as jnp
from jax import lax
from jax.experimental import pallas as pl
from jax.experimental.pallas import tpu as pltpu
from jax.sharding import PartitionSpec as P

HEADS = 8
HDIM = 32
GRID = 8
SEG = 16
PITCH = 72
MESH = pl.DeviceIdType.MESH
BF = jnp.bfloat16
F32 = jnp.float32


def sigmoid(t):
    return 0.5 * jnp.tanh(0.5 * t) + 0.5


def layer_norm(values):
    center = values - jnp.mean(values, axis=-1, keepdims=True)
    spread = jnp.mean(center * center, axis=-1, keepdims=True)
    return center * lax.rsqrt(spread + 1e-05)


def shifted_row(a_ref, row, cells, lane):
    count, width = cells.shape
    wide = cells.astype(F32)
    a_ref[row, :, lane : lane + width] = pltpu.roll(wide, 1, 0).astype(BF)
    a_ref[row, :, lane + width : lane + 2 * width] = cells
    a_ref[row, :, lane + 2 * width : lane + 3 * width] = pltpu.roll(wide, count - 1, 0).astype(BF)


def patch_row(a_ref, row, left, right, lane):
    cols, width = a_ref.shape[1], left.shape[1]
    pos = lax.broadcasted_iota(jnp.int32, (SEG, width), 0)
    tile = a_ref[row, 0:SEG, lane : lane + width].astype(F32)
    a_ref[row, 0:SEG, lane : lane + width] = jnp.where(pos == 0, left, tile).astype(BF)
    lane += 2 * width
    tile = a_ref[row, cols - SEG : cols, lane : lane + width].astype(F32)
    a_ref[row, cols - SEG : cols, lane : lane + width] = jnp.where(pos == SEG - 1, right, tile).astype(BF)


def window(a_ref, row, rows, col, cols, low, high):
    taps = [a_ref[pl.ds(row + a, rows), col : col + cols, low:high].reshape(rows * cols, high - low) for a in range(3)]
    return jnp.concatenate(taps, axis=1)


def gates_of(a_ref, w_ref, row, rows, col, cols, split):
    depth = a_ref.shape[2]
    taps = jnp.concatenate(
        [window(a_ref, row, rows, col, cols, 0, split), window(a_ref, row, rows, col, cols, split, depth)], axis=1
    )
    return jnp.dot(taps, w_ref[...], preferred_element_type=F32)


def lstm(gates, cell):
    width = cell.shape[1]
    new_cell = sigmoid(gates[:, width : 2 * width]) * cell + sigmoid(gates[:, :width]) * jnp.tanh(
        gates[:, 2 * width : 3 * width]
    )
    return new_cell, sigmoid(gates[:, 3 * width :]) * jnp.tanh(new_cell)


def peer(j, parity, columns):
    return {"gy": 2 * (j // columns) + parity, "gx": j % columns}


class Shift:
    def __init__(self, src, dst, dy, dx, send_sem, recv_sem):
        gy, gx = lax.axis_index("gy"), lax.axis_index("gx")
        ny, nx = lax.axis_size("gy"), lax.axis_size("gx")

        def inside(y, x):
            return jnp.logical_and(jnp.logical_and(y >= 0, y < ny), jnp.logical_and(x >= 0, x < nx))

        self.dst = dst
        self.to = inside(gy + dy, gx + dx)
        self.come = inside(gy - dy, gx - dx)
        self.copy = pltpu.make_async_remote_copy(
            src_ref=src,
            dst_ref=dst,
            send_sem=send_sem,
            recv_sem=recv_sem,
            device_id={"gy": gy + dy, "gx": gx + dx},
            device_id_type=MESH,
        )

    def clear(self):
        @pl.when(jnp.logical_not(self.come))
        def _():
            self.dst[...] = jnp.zeros(self.dst.shape, self.dst.dtype)

    def start(self):
        @pl.when(self.to)
        def _():
            self.copy.start()

    def wait_recv(self):
        @pl.when(self.come)
        def _():
            self.copy.wait_recv()

    def wait_send(self):
        @pl.when(self.to)
        def _():
            self.copy.wait_send()


def shifts(pieces, cols_out, cols_in, corners_out, corners_in, send_sems, recv_sems):
    plan = []

    def add(src, dst, dy, dx):
        at = len(plan)
        plan.append(Shift(src, dst, dy, dx, send_sems.at[at], recv_sems.at[at]))

    for side, dx in ((1, -1), (0, 1)):
        add(cols_out.at[1 - side], cols_in.at[side], 0, dx)
    for dy, low in ((-1, 2), (1, 0)):
        for dx, side in ((-1, 1), (1, 0)):
            add(corners_out.at[3 - low - side], corners_in.at[low + side], dy, dx)
    for cells, rows_in in pieces:
        rows = cells.shape[0]
        add(cells.at[0], rows_in.at[1], -1, 0)
        add(cells.at[rows - 1], rows_in.at[0], 1, 0)
    return plan


def edge_columns(cells, cols_out, scratch, lane):
    rows, cols, width = cells.shape

    def eight(i, _):
        base = pl.multiple_of(i * 8, 8)
        low = [cells[base + k, 0:SEG, :].astype(F32)[0:1] for k in range(8)]
        high = [cells[base + k, cols - SEG : cols, :].astype(F32)[SEG - 1 : SEG] for k in range(8)]
        scratch[0, pl.ds(base, 8), lane : lane + width] = jnp.concatenate(low, axis=0)
        scratch[1, pl.ds(base, 8), lane : lane + width] = jnp.concatenate(high, axis=0)
        return 0

    lax.fori_loop(0, rows // 8, eight, 0)
    cols_out[:, :, lane : lane + width] = scratch[:, 0:rows, lane : lane + width].astype(BF)


def edge_corners(cells, corners_out, lane):
    rows, cols, width = cells.shape
    for k in range(4):
        row = (k // 2) * (rows - 1)
        if k % 2:
            cell = cells[row, cols - SEG : cols, :].astype(F32)[SEG - 1 : SEG]
        else:
            cell = cells[row, 0:SEG, :].astype(F32)[0:1]
        corners_out[k, :, lane : lane + width] = cell


def head_mask():
    row = lax.broadcasted_iota(jnp.int32, (256, 256), 0)
    col = lax.broadcasted_iota(jnp.int32, (256, 256), 1)
    heads = ((col % 128) // HDIM == row // 64).astype(F32).astype(BF)
    blocks = (col // 64 == row // 64).astype(F32).astype(BF)
    return heads, blocks


def attend_chunk(tokens, w_qkv, w_out, heads, blocks, wide, qkv, prob, outs):
    members = tokens.shape[0]
    cells = members * SEG
    wide[0:cells, :] = tokens.reshape(cells, 128).astype(F32)
    grouped = jnp.concatenate([wide[pl.ds(g, members, stride=SEG), :] for g in range(SEG)], axis=0).astype(BF)
    qkv[...] = jnp.dot(grouped, w_qkv[...], preferred_element_type=F32).astype(BF)
    zero = jnp.zeros((64, 128), BF)

    def spread(base, lane):
        pair = jnp.concatenate([qkv[base : base + 64, lane : lane + 128], qkv[base + 64 : base + 128, lane : lane + 128]], axis=1)
        return jnp.concatenate([pair] * 4, axis=0) * heads

    for base in range(0, cells, 128):
        for half in range(2):
            lane = half * 128
            q1 = jnp.concatenate([qkv[base : base + 64, lane : lane + 128], zero], axis=1)
            q2 = jnp.concatenate([zero, qkv[base + 64 : base + 128, lane : lane + 128]], axis=1)
            s = lax.dot_general(
                jnp.concatenate([q1, q2], axis=0),
                spread(base, 256 + lane),
                (((1,), (1,)), ((), ())),
                preferred_element_type=F32,
            )
            prob[half, base : base + 128, :] = jnp.minimum(jnp.exp(s * HDIM**-0.5), 3.3895e38).astype(BF)
    step = 512
    for base in range(0, cells, step):
        for half in range(2):
            raised = prob[half, base : base + step, :]
            total = jnp.dot(raised, blocks, preferred_element_type=F32)
            prob[half, base : base + step, :] = (raised.astype(F32) * (1.0 / total)).astype(BF)
    for base in range(0, cells, 128):
        for half in range(2):
            lane = half * 128
            o = jnp.dot(prob[half, base : base + 128, :], spread(base, 512 + lane), preferred_element_type=F32)
            outs[base : base + 64, lane : lane + 128] = o[:64, :128].astype(BF)
            outs[base + 64 : base + 128, lane : lane + 128] = o[64:, 128:].astype(BF)
    done = jnp.dot(outs[...], w_out[...], preferred_element_type=F32)
    for g in range(SEG):
        wide[g * PITCH : g * PITCH + members, :] = done[g * members : (g + 1) * members]


def mlp_rows(hidden, attended, w_up, w_down):
    mixed = hidden.astype(F32) + attended.astype(F32)
    normed = layer_norm(mixed).astype(BF)
    u = jnp.dot(normed, w_up[...], preferred_element_type=F32)
    twice = u + u * jnp.tanh(u * (0.7978845608 + 0.7978845608 * 0.044715 * (u * u)))
    return (mixed + 0.5 * jnp.dot(twice.astype(BF), w_down[...], preferred_element_type=F32)).astype(BF)


def kernel(*refs):
    names = iter(refs)
    take = lambda n: [next(names) for _ in range(n)]
    frames, hidden, cell, w_gates, bias_in, wqkv_in, wout_in, wup_in, wdown_in = take(9)
    block_out, cell_out = take(2)
    f1, f2, hd, cl, w, bias_v, w_qkv, w_out, w_up, w_down = take(10)
    a1, a2, h1, h2, normed, tok, ret, land, outb = take(9)
    rows_a, rows_h, cols_out, cols_in, corn_out, corn_in, edge = take(7)
    rows_b, cols_out_b, cols_in_b, corn_out_b, corn_in_b, edge_b = take(6)
    rows_1, cols_out_1, cols_in_1, corn_out_1, corn_in_1, edge_1 = take(6)
    part, wide, qkv, prob, outs = take(5)
    load_sem, send_a, recv_a, send_b, recv_b, send_1, recv_1, to_send, to_recv, back_send, back_recv, out_sem = take(12)

    rows, cols, width = hd.shape
    latent = f1.shape[2]
    gy, gx = lax.axis_index("gy"), lax.axis_index("gx")
    ny, nx = lax.axis_size("gy"), lax.axis_size("gx")
    parity = gy % 2
    count = ny // 2 * nx
    me = (gy // 2) * nx + gx
    split = 3 * latent
    step = 8
    groups = rows // step

    used = iter(range(64))

    def load(src, dst):
        return pltpu.make_async_copy(src, dst, load_sem.at[next(used)])

    first_loads = []
    for g in range(groups):
        at = pl.ds(g * step, step)
        first_loads.append((load(frames.at[at, :, pl.ds(0, latent)], f1.at[at]), load(hidden.at[at], hd.at[at])))
    gate_loads = []
    for a in range(3):
        for b in range(3):
            at = (a * 3 + b) * latent
            gate_loads.append(load(w_gates.at[a, b, pl.ds(0, latent)], w.at[pl.ds(at, latent)]))
            at = 9 * latent + (a * 3 + b) * width
            gate_loads.append(load(w_gates.at[a, b, pl.ds(latent, width)], w.at[pl.ds(at, width)]))
    gate_loads += [load(cell, cl), load(bias_in, bias_v)]
    load_f2 = load(frames.at[:, :, pl.ds(latent, latent)], f2)
    late_loads = [load(wqkv_in, w_qkv), load(wout_in, w_out), load(wup_in, w_up), load(wdown_in, w_down)]

    halo_a = shifts(((f1, rows_a), (hd, rows_h)), cols_out, cols_in, corn_out, corn_in, send_a, recv_a)
    halo_b = shifts(((f2, rows_b),), cols_out_b, cols_in_b, corn_out_b, corn_in_b, send_b, recv_b)
    halo_1 = shifts(((h1, rows_1),), cols_out_1, cols_in_1, corn_out_1, corn_in_1, send_1, recv_1)

    for pair in first_loads:
        for copy in pair:
            copy.start()
    barrier = pltpu.get_barrier_semaphore()

    def greet(i, _):
        pl.semaphore_signal(barrier, inc=1, device_id=peer((me + i) % count, parity, nx), device_id_type=MESH)
        return 0

    lax.fori_loop(1, count, greet, 0)
    greeted = count - 1
    for dy in (-1, 1):
        for dx in (-1, 0, 1):
            y, x = gy + dy, gx + dx
            near = jnp.logical_and(jnp.logical_and(y >= 0, y < ny), jnp.logical_and(x >= 0, x < nx))

            @pl.when(near)
            def _():
                pl.semaphore_signal(barrier, inc=1, device_id={"gy": y, "gx": x}, device_id_type=MESH)

            greeted = greeted + near.astype(jnp.int32)
    for copy in gate_loads + [load_f2] + late_loads:
        copy.start()
    for shift in halo_a + halo_b + halo_1:
        shift.clear()

    for g in range(groups):
        for copy in first_loads[g]:
            copy.wait()

        def build(r, _):
            shifted_row(a1, r + 1, f1[r], 0)
            shifted_row(a1, r + 1, hd[r], split)
            return 0

        lax.fori_loop(g * step, g * step + step, build, 0)
    edge_columns(f1, cols_out, edge, 0)
    edge_columns(hd, cols_out, edge, latent)
    edge_corners(f1, corn_out, 0)
    edge_corners(hd, corn_out, latent)
    for copy in gate_loads:
        copy.wait()
    bias = bias_v[...]

    def step_one(row, count_r, col, count_c):
        cells = count_r * count_c
        old = cl[pl.ds(row, count_r), col : col + count_c, :].reshape(cells, width)
        new_cell, hid = lstm(gates_of(a1, w, row, count_r, col, count_c, split) + bias, old)
        cl[pl.ds(row, count_r), col : col + count_c, :] = new_cell.reshape(count_r, count_c, width)
        h1[pl.ds(row, count_r), col : col + count_c, :] = hid.astype(BF).reshape(count_r, count_c, width)

    step_one(8, 16, SEG, cols - 2 * SEG)
    load_f2.wait()
    edge_columns(f2, cols_out_b, edge_b, 0)
    edge_corners(f2, corn_out_b, 0)
    pl.semaphore_wait(barrier, greeted)
    for shift in halo_a + halo_b:
        shift.start()
    step_one(24, 16, SEG, cols - 2 * SEG)

    def build_two(r, _):
        shifted_row(a2, r + 1, f2[r], 0)
        return 0

    lax.fori_loop(0, rows, build_two, 0, unroll=2)

    def patch(a_ref, side_in, parts):
        def eight(i, _):
            base = pl.multiple_of(i * 8, 8)
            left, right = side_in[0, pl.ds(base, 8), :], side_in[1, pl.ds(base, 8), :]
            for k in range(8):
                for low, high, lane in parts:
                    patch_row(a_ref, base + k + 1, left[k : k + 1, low:high], right[k : k + 1, low:high], lane)
            return 0

        lax.fori_loop(0, rows // 8, eight, 0)

    def outer(a_ref, rows_in, corners, low, lane):
        high = low + rows_in.shape[2]
        for end, row in ((0, 0), (1, rows + 1)):
            shifted_row(a_ref, row, rows_in[end], lane)
            patch_row(a_ref, row, corners[2 * end, :, low:high], corners[2 * end + 1, :, low:high], lane)

    for shift in halo_a:
        shift.wait_recv()
    edge[...] = cols_in[...].astype(F32)
    patch(a1, edge, ((0, latent, 0), (latent, latent + width, split)))
    outer(a1, rows_a, corn_in, 0, 0)
    outer(a1, rows_h, corn_in, latent, split)

    step_one(0, 8, 0, cols)
    step_one(rows - 8, 8, 0, cols)
    step_one(8, 32, 0, SEG)
    step_one(8, 32, cols - SEG, SEG)
    edge_columns(h1, cols_out_1, edge_1, 0)
    edge_corners(h1, corn_out_1, 0)
    for shift in halo_1:
        shift.start()
    for shift in halo_b:
        shift.wait_recv()
    edge_b[...] = cols_in_b[...].astype(F32)
    patch(a2, edge_b, ((0, latent, 0),))
    outer(a2, rows_b, corn_in_b, 0, 0)

    def build_three(r, _):
        shifted_row(a2, r + 1, h1[r], split)
        return 0

    lax.fori_loop(0, rows, build_three, 0, unroll=2)
    early = part.shape[0]
    for s in range(early):
        part[s] = (
            jnp.dot(window(a2, s * step, step, 0, cols, 0, split), w[0 : 9 * latent], preferred_element_type=F32) + bias
        )
    for shift in halo_1:
        shift.wait_recv()
    edge_1[...] = cols_in_1[...].astype(F32)
    patch(a2, edge_1, ((0, width, split),))
    outer(a2, rows_1, corn_in_1, 0, split)

    quarters = cols // SEG
    sent = step * quarters

    def forward(j, c):
        return pltpu.make_async_remote_copy(
            src_ref=normed.at[c * count + j],
            dst_ref=tok.at[c, me],
            send_sem=to_send,
            recv_sem=to_recv.at[c],
            device_id=peer(j, parity, nx),
            device_id_type=MESH,
        )

    def send_forward(s):
        c, half = s * sent // count, s * sent % count
        for t in range(1, sent):
            forward(half + (me + t) % sent, c).start()

    def send_last(s):
        c, half = s * sent // count, s * sent % count

        @pl.when(me // sent != half // sent)
        def _():
            forward(half + me % sent, c).start()

    def step_two(s):
        row = s * step
        cells = step * cols
        if s < early:
            hidden_taps = window(a2, row, step, 0, cols, split, a2.shape[2])
            gates = part[s] + jnp.dot(hidden_taps, w[9 * latent :], preferred_element_type=F32)
        else:
            gates = gates_of(a2, w, row, step, 0, cols, split) + bias
        new_cell, hid = lstm(gates, cl[pl.ds(row, step)].reshape(cells, width))
        cl[pl.ds(row, step)] = new_cell.reshape(step, cols, width)
        hid = hid.astype(BF)
        h2[pl.ds(row * quarters, sent)] = hid.reshape(sent, SEG, width)
        normed[pl.ds(row * quarters, sent)] = layer_norm(hid.astype(F32)).astype(BF).reshape(sent, SEG, width)
        pltpu.make_async_copy(cl.at[pl.ds(row, step)], cell_out.at[pl.ds(row, step)], out_sem.at[0]).start()

    for s in range(groups):
        if s:
            send_last(s - 1)
            send_forward(s - 1)
        step_two(s)
    for copy in late_loads:
        copy.wait()
    heads, blocks = head_mask()
    chunks = tok.shape[0]

    def wait_for(ref, sem):
        pltpu.make_async_remote_copy(
            src_ref=ref, dst_ref=ref, send_sem=to_send, recv_sem=sem, device_id=peer(me, parity, nx), device_id_type=MESH
        ).wait_recv()

    def send_back(c):
        for t in range(1, count):
            m = (me + t) % count
            pltpu.make_async_remote_copy(
                src_ref=ret.at[c, m],
                dst_ref=land.at[c * count + me],
                send_sem=back_send,
                recv_sem=back_recv.at[c],
                device_id=peer(m, parity, nx),
                device_id_type=MESH,
            ).start()

    for c in range(chunks):
        tok[c, me] = normed[c * count + me]
        if c == 0:
            send_last(groups - 1)
        wait_for(tok.at[c, pl.ds(0, count - 1)], to_recv.at[c])
        if c == 0:
            send_forward(groups - 1)
        else:
            send_back(c - 1)
        attend_chunk(tok[c], w_qkv, w_out, heads, blocks, wide, qkv, prob, outs)
        for m in range(count):
            ret[c, m] = wide[pl.ds(m, SEG, stride=PITCH), :].astype(BF)
        land[c * count + me] = ret[c, me]
    send_back(chunks - 1)
    for c in range(chunks):
        base = c * count
        wait_for(land.at[pl.ds(base, count - 1)], back_recv.at[c])
        cells = count * SEG
        result = mlp_rows(
            h2[pl.ds(base, count)].reshape(cells, width), land[pl.ds(base, count)].reshape(cells, width), w_up, w_down
        )
        outb[pl.ds(c * SEG, SEG)] = result.reshape(SEG, cols, width)
        pltpu.make_async_copy(outb.at[pl.ds(c * SEG, SEG)], block_out.at[pl.ds(c * SEG, SEG)], out_sem.at[1]).start()
    for shift in halo_a + halo_b + halo_1:
        shift.wait_send()
    for sem, source in ((to_send, tok), (back_send, ret)):
        most = source.at[:, pl.ds(0, count - 1)]
        pltpu.make_async_remote_copy(
            src_ref=most, dst_ref=most, send_sem=sem, recv_sem=to_recv.at[0],
            device_id=peer(me, parity, nx), device_id_type=MESH,
        ).wait_send()
    pltpu.make_async_copy(cl, cell_out, out_sem.at[0]).wait()
    pltpu.make_async_copy(outb, block_out, out_sem.at[1]).wait()


def body(frames, hidden_state, cell_state, w_gates, gate_bias, w_qkv, w_out, w_up, w_down):
    rows, cols, width = hidden_state.shape
    latent = frames.shape[2] // 2
    gates = w_gates.shape[3]
    depth = 3 * (latent + width)
    members = lax.axis_size("gy") // 2 * lax.axis_size("gx")
    chunks = rows * cols // (members * SEG)
    cells = members * SEG
    any_space = pl.BlockSpec(memory_space=pl.ANY)
    dma = pltpu.SemaphoreType.DMA

    def vm(*shape, dtype=BF):
        return pltpu.VMEM(shape, dtype)

    def sides(span):
        return [
            vm(2, rows, span), vm(2, rows, span), vm(4, 1, span, dtype=F32), vm(4, 1, span, dtype=F32),
            vm(2, rows, span, dtype=F32),
        ]

    scratch = [
        vm(rows, cols, latent), vm(rows, cols, latent), vm(rows, cols, width), vm(rows, cols, width, dtype=F32),
        vm(3 * depth, gates), vm(1, gates, dtype=F32), vm(*w_qkv.shape), vm(*w_out.shape), vm(*w_up.shape),
        vm(*w_down.shape),
        vm(rows + 2, cols, depth), vm(rows + 2, cols, depth), vm(rows, cols, width),
        vm(chunks * members, SEG, width), vm(chunks * members, SEG, width),
        vm(chunks, members, SEG, width), vm(chunks, members, SEG, width),
        vm(chunks * members, SEG, width), vm(rows, cols, width),
        vm(2, cols, latent), vm(2, cols, width), *sides(latent + width),
        vm(2, cols, latent), *sides(latent),
        vm(2, cols, width), *sides(width),
        vm(2, 8 * cols, gates, dtype=F32),
        vm(SEG * PITCH, width, dtype=F32), vm(cells, 3 * HEADS * HDIM), vm(2, cells, 256), vm(cells, HEADS * HDIM),
        dma((64,)), dma((10,)), dma((10,)), dma((8,)), dma((8,)), dma((8,)), dma((8,)),
        dma, dma((chunks,)), dma, dma((chunks,)), dma((2,)),
    ]
    return pl.pallas_call(
        kernel,
        out_shape=(jax.ShapeDtypeStruct(hidden_state.shape, BF), jax.ShapeDtypeStruct(cell_state.shape, F32)),
        in_specs=[any_space] * 9,
        out_specs=[any_space] * 2,
        scratch_shapes=scratch,
        compiler_params=pltpu.CompilerParams(vmem_limit_bytes=60 * 2**20, collective_id=1, has_side_effects=True),
        name="fused",
    )(frames, hidden_state, cell_state, w_gates, gate_bias[None], w_qkv, w_out, w_up, w_down)


def solution(mesh):
    spec = P("gy", "gx", None)
    return jax.shard_map(
        body,
        mesh=mesh,
        in_specs=(spec, spec, spec, P(), P(), P(), P(), P(), P()),
        out_specs=(spec, spec),
        check_vma=False,
    )
```

```python
import jax
import jax.numpy as jnp
from jax import lax
from jax.experimental import pallas as pl
from jax.experimental.pallas import tpu as pltpu
from jax.sharding import PartitionSpec as P

HEADS = 8
HDIM = 32
GRID = 8
SEG = 16
PITCH = 72
SIDE = 4
MESH = pl.DeviceIdType.MESH
BF = jnp.bfloat16
F32 = jnp.float32


def sigmoid(t):
    return 0.5 * jnp.tanh(0.5 * t) + 0.5


def layer_norm(values):
    center = values - jnp.mean(values, axis=-1, keepdims=True)
    spread = jnp.mean(center * center, axis=-1, keepdims=True)
    return center * lax.rsqrt(spread + 1e-05)


def shifted_row(a_ref, row, cells, lane):
    count, width = cells.shape
    wide = cells.astype(F32)
    a_ref[row, :, lane : lane + width] = pltpu.roll(wide, 1, 0).astype(BF)
    a_ref[row, :, lane + width : lane + 2 * width] = cells
    a_ref[row, :, lane + 2 * width : lane + 3 * width] = pltpu.roll(wide, count - 1, 0).astype(BF)


def patch_row(a_ref, row, left, right, lane):
    cols, width = a_ref.shape[1], left.shape[1]
    pos = lax.broadcasted_iota(jnp.int32, (SEG, width), 0)
    tile = a_ref[row, 0:SEG, lane : lane + width].astype(F32)
    a_ref[row, 0:SEG, lane : lane + width] = jnp.where(pos == 0, left, tile).astype(BF)
    lane += 2 * width
    tile = a_ref[row, cols - SEG : cols, lane : lane + width].astype(F32)
    a_ref[row, cols - SEG : cols, lane : lane + width] = jnp.where(pos == SEG - 1, right, tile).astype(BF)


def window(a_ref, row, rows, col, cols, low, high):
    taps = [a_ref[pl.ds(row + a, rows), col : col + cols, low:high].reshape(rows * cols, high - low) for a in range(3)]
    return jnp.concatenate(taps, axis=1)


def rows_of(w_ref):
    return w_ref[...].reshape(-1, w_ref.shape[3])


def whole(w_refs):
    return jnp.concatenate([rows_of(w) for w in w_refs], axis=0)


def gates_of(a_ref, w_ref, row, rows, col, cols, split):
    depth = a_ref.shape[2]
    taps = jnp.concatenate(
        [window(a_ref, row, rows, col, cols, 0, split), window(a_ref, row, rows, col, cols, split, depth)], axis=1
    )
    return jnp.dot(taps, whole(w_ref), preferred_element_type=F32)


def lstm(gates, cell):
    width = cell.shape[1]
    new_cell = sigmoid(gates[:, width : 2 * width]) * cell + sigmoid(gates[:, :width]) * jnp.tanh(
        gates[:, 2 * width : 3 * width]
    )
    return new_cell, sigmoid(gates[:, 3 * width :]) * jnp.tanh(new_cell)


def far_first(steps):
    return sorted(steps, key=lambda d: (-sum(min(v, SIDE - v) for v in d), sum(d) % 3, d))


class Torus:
    def __init__(self):
        gy, gx = lax.axis_index("gy"), lax.axis_index("gx")
        self.here = {"gy": gy, "gx": gx}
        self.parity = gy % 2
        k = gy // 2
        low, high, x, y = k // SIDE, gx % 2, gx // 2, k % SIDE
        self.low = low
        self.xs = [(x + d) % SIDE * 2 for d in range(SIDE)]
        self.ys = [(y + d) % SIDE for d in range(SIDE)]
        z = high * 2 + low
        self.zs = [((z + d) % SIDE % 2 * SIDE, (z + d) % SIDE // 2) for d in range(SIDE)]
        self.highs = [high, (high + 1) % 2]
        self.me = k * 2 * SIDE + gx

    def at(self, k, gx):
        return k * 2 * SIDE + gx, {"gy": 2 * k + self.parity, "gx": gx}

    def others(self):
        steps = [(a, b, c) for a in range(SIDE) for b in range(SIDE) for c in range(SIDE) if a or b or c]
        for a, b, c in far_first(steps):
            yield self.at(self.zs[c][0] + self.ys[b], self.xs[a] + self.zs[c][1])

    def half(self, low):
        steps = [(a, b, 2 * c) for a in range(SIDE) for b in range(SIDE) for c in range(2) if a or b or c]
        for a, b, c in far_first(steps):
            yield self.at(low * SIDE + self.ys[b], self.xs[a] + self.highs[c // 2])

    def mine(self, low):
        return self.at(low * SIDE + self.ys[0], self.xs[0] + self.highs[0])


class Shift:
    def __init__(self, src, dst, dy, dx, send_sem, recv_sem):
        gy, gx = lax.axis_index("gy"), lax.axis_index("gx")
        ny, nx = lax.axis_size("gy"), lax.axis_size("gx")

        def inside(y, x):
            return jnp.logical_and(jnp.logical_and(y >= 0, y < ny), jnp.logical_and(x >= 0, x < nx))

        self.dst = dst
        self.to = inside(gy + dy, gx + dx)
        self.come = inside(gy - dy, gx - dx)
        self.copy = pltpu.make_async_remote_copy(
            src_ref=src,
            dst_ref=dst,
            send_sem=send_sem,
            recv_sem=recv_sem,
            device_id={"gy": gy + dy, "gx": gx + dx},
            device_id_type=MESH,
        )

    def clear(self):
        @pl.when(jnp.logical_not(self.come))
        def _():
            self.dst[...] = jnp.zeros(self.dst.shape, self.dst.dtype)

    def start(self):
        @pl.when(self.to)
        def _():
            self.copy.start()

    def wait_recv(self):
        @pl.when(self.come)
        def _():
            self.copy.wait_recv()

    def wait_send(self):
        @pl.when(self.to)
        def _():
            self.copy.wait_send()


def shifts(pieces, cols_out, cols_in, corners_out, corners_in, send_sems, recv_sems):
    plan = []

    def add(src, dst, dy, dx):
        at = len(plan)
        plan.append(Shift(src, dst, dy, dx, send_sems.at[at], recv_sems.at[at]))

    for side, dx in ((1, -1), (0, 1)):
        add(cols_out.at[1 - side], cols_in.at[side], 0, dx)
    for dy, low in ((-1, 2), (1, 0)):
        for dx, side in ((-1, 1), (1, 0)):
            add(corners_out.at[3 - low - side], corners_in.at[low + side], dy, dx)
    for cells, rows_in in pieces:
        rows = cells.shape[0]
        add(cells.at[0], rows_in.at[1], -1, 0)
        add(cells.at[rows - 1], rows_in.at[0], 1, 0)
    return plan


def edge_columns(cells, cols_out, scratch, lane):
    rows, cols, width = cells.shape

    def eight(i, _):
        base = pl.multiple_of(i * 8, 8)
        low = [cells[base + k, 0:SEG, :].astype(F32)[0:1] for k in range(8)]
        high = [cells[base + k, cols - SEG : cols, :].astype(F32)[SEG - 1 : SEG] for k in range(8)]
        scratch[0, pl.ds(base, 8), lane : lane + width] = jnp.concatenate(low, axis=0)
        scratch[1, pl.ds(base, 8), lane : lane + width] = jnp.concatenate(high, axis=0)
        return 0

    lax.fori_loop(0, rows // 8, eight, 0)
    cols_out[:, :, lane : lane + width] = scratch[:, 0:rows, lane : lane + width].astype(BF)


def edge_corners(cells, corners_out, lane):
    rows, cols, width = cells.shape
    for k in range(4):
        row = (k // 2) * (rows - 1)
        if k % 2:
            cell = cells[row, cols - SEG : cols, :].astype(F32)[SEG - 1 : SEG]
        else:
            cell = cells[row, 0:SEG, :].astype(F32)[0:1]
        corners_out[k, :, lane : lane + width] = cell


def head_mask():
    row = lax.broadcasted_iota(jnp.int32, (256, 256), 0)
    col = lax.broadcasted_iota(jnp.int32, (256, 256), 1)
    heads = ((col % 128) // HDIM == row // 64).astype(F32).astype(BF)
    blocks = (col // 64 == row // 64).astype(F32).astype(BF)
    return heads, blocks


def attend_chunk(tokens, w_qkv, w_out, heads, blocks, wide, qkv, prob, outs):
    members = tokens.shape[0]
    cells = members * SEG
    wide[0:cells, :] = tokens.reshape(cells, 128).astype(F32)
    grouped = jnp.concatenate([wide[pl.ds(g, members, stride=SEG), :] for g in range(SEG)], axis=0).astype(BF)
    qkv[...] = jnp.dot(grouped, w_qkv[...], preferred_element_type=F32).astype(BF)
    zero = jnp.zeros((64, 128), BF)

    def spread(base, lane):
        pair = jnp.concatenate([qkv[base : base + 64, lane : lane + 128], qkv[base + 64 : base + 128, lane : lane + 128]], axis=1)
        return jnp.concatenate([pair] * 4, axis=0) * heads

    for base in range(0, cells, 128):
        for half in range(2):
            lane = half * 128
            q1 = jnp.concatenate([qkv[base : base + 64, lane : lane + 128], zero], axis=1)
            q2 = jnp.concatenate([zero, qkv[base + 64 : base + 128, lane : lane + 128]], axis=1)
            s = lax.dot_general(
                jnp.concatenate([q1, q2], axis=0),
                spread(base, 256 + lane),
                (((1,), (1,)), ((), ())),
                preferred_element_type=F32,
            )
            prob[half, base : base + 128, :] = jnp.minimum(jnp.exp(s * HDIM**-0.5), 3.3895e38).astype(BF)
    step = 512
    for base in range(0, cells, step):
        for half in range(2):
            raised = prob[half, base : base + step, :]
            total = jnp.dot(raised, blocks, preferred_element_type=F32)
            prob[half, base : base + step, :] = (raised.astype(F32) * (1.0 / total)).astype(BF)
    for base in range(0, cells, 128):
        for half in range(2):
            lane = half * 128
            o = jnp.dot(prob[half, base : base + 128, :], spread(base, 512 + lane), preferred_element_type=F32)
            outs[base : base + 64, lane : lane + 128] = o[:64, :128].astype(BF)
            outs[base + 64 : base + 128, lane : lane + 128] = o[64:, 128:].astype(BF)
    done = jnp.dot(outs[...], w_out[...], preferred_element_type=F32)
    for g in range(SEG):
        wide[g * PITCH : g * PITCH + members, :] = done[g * members : (g + 1) * members]


def mlp_rows(hidden, attended, w_up, w_down):
    mixed = hidden.astype(F32) + attended.astype(F32)
    normed = layer_norm(mixed).astype(BF)
    u = jnp.dot(normed, w_up[...], preferred_element_type=F32)
    twice = u + u * jnp.tanh(u * (0.7978845608 + 0.7978845608 * 0.044715 * (u * u)))
    return (mixed + 0.5 * jnp.dot(twice.astype(BF), w_down[...], preferred_element_type=F32)).astype(BF)


def kernel(*refs):
    names = iter(refs)
    take = lambda n: [next(names) for _ in range(n)]
    frames, hidden, cell, w_gates, bias_in, wqkv_in, wout_in, wup_in, wdown_in = take(9)
    block_out, cell_out = take(2)
    f1, f2, hd, cl, w_f, w_h, bias_v, w_qkv, w_out, w_up, w_down = take(11)
    w = (w_f, w_h)
    a1, a2, h1, h2, normed, tok, ret, land, outb = take(9)
    rows_a, rows_h, cols_out, cols_in, corn_out, corn_in, edge = take(7)
    rows_b, cols_out_b, cols_in_b, corn_out_b, corn_in_b, edge_b = take(6)
    rows_1, cols_out_1, cols_in_1, corn_out_1, corn_in_1, edge_1 = take(6)
    part, wide, qkv, prob, outs = take(5)
    load_sem, send_a, recv_a, send_b, recv_b, send_1, recv_1, to_send, to_recv, back_send, back_recv, out_sem = take(12)

    rows, cols, width = hd.shape
    latent = f1.shape[2]
    torus = Torus()
    gy, gx = torus.here["gy"], torus.here["gx"]
    ny, nx = lax.axis_size("gy"), lax.axis_size("gx")
    count = ny // 2 * nx
    me = torus.me
    split = 3 * latent
    step = 8
    groups = rows // step

    used = iter(range(64))

    def load(src, dst):
        return pltpu.make_async_copy(src, dst, load_sem.at[next(used)])

    first_loads = []
    bunch = 2 * step
    for row in range(0, rows, bunch):
        at = pl.ds(row, bunch)
        first_loads.append((load(frames.at[at, :, pl.ds(0, latent)], f1.at[at]), load(hidden.at[at], hd.at[at])))
    gate_loads = [
        load(w_gates.at[:, :, pl.ds(0, latent)], w_f),
        load(w_gates.at[:, :, pl.ds(latent, width)], w_h),
        load(cell, cl),
        load(bias_in, bias_v),
    ]
    load_f2 = load(frames.at[:, :, pl.ds(latent, latent)], f2)
    late_loads = [load(wqkv_in, w_qkv), load(wout_in, w_out), load(wup_in, w_up), load(wdown_in, w_down)]

    halo_a = shifts(((f1, rows_a), (hd, rows_h)), cols_out, cols_in, corn_out, corn_in, send_a, recv_a)
    halo_b = shifts(((f2, rows_b),), cols_out_b, cols_in_b, corn_out_b, corn_in_b, send_b, recv_b)
    halo_1 = shifts(((h1, rows_1),), cols_out_1, cols_in_1, corn_out_1, corn_in_1, send_1, recv_1)

    for pair in first_loads:
        for copy in pair:
            copy.start()
    barrier = pltpu.get_barrier_semaphore()

    for _, device in torus.others():
        pl.semaphore_signal(barrier, inc=1, device_id=device, device_id_type=MESH)
    greeted = count - 1
    for dy in (-1, 1):
        for dx in (-1, 0, 1):
            y, x = gy + dy, gx + dx
            near = jnp.logical_and(jnp.logical_and(y >= 0, y < ny), jnp.logical_and(x >= 0, x < nx))

            @pl.when(near)
            def _():
                pl.semaphore_signal(barrier, inc=1, device_id={"gy": y, "gx": x}, device_id_type=MESH)

            greeted = greeted + near.astype(jnp.int32)
    for copy in gate_loads + [load_f2] + late_loads:
        copy.start()
    for shift in halo_a + halo_b + halo_1:
        shift.clear()

    for g, pair in enumerate(first_loads):
        for copy in pair:
            copy.wait()

        def build(r, _):
            shifted_row(a1, r + 1, f1[r], 0)
            shifted_row(a1, r + 1, hd[r], split)
            return 0

        lax.fori_loop(g * bunch, g * bunch + bunch, build, 0, unroll=2)
    edge_columns(f1, cols_out, edge, 0)
    edge_columns(hd, cols_out, edge, latent)
    edge_corners(f1, corn_out, 0)
    edge_corners(hd, corn_out, latent)
    pl.semaphore_wait(barrier, greeted)
    for shift in halo_a:
        shift.start()
    for copy in gate_loads:
        copy.wait()
    bias = bias_v[...]

    def step_one(row, count_r, col, count_c):
        cells = count_r * count_c
        old = cl[pl.ds(row, count_r), col : col + count_c, :].reshape(cells, width)
        new_cell, hid = lstm(gates_of(a1, w, row, count_r, col, count_c, split) + bias, old)
        cl[pl.ds(row, count_r), col : col + count_c, :] = new_cell.reshape(count_r, count_c, width)
        h1[pl.ds(row, count_r), col : col + count_c, :] = hid.astype(BF).reshape(count_r, count_c, width)

    step_one(8, 16, SEG, cols - 2 * SEG)
    load_f2.wait()
    edge_columns(f2, cols_out_b, edge_b, 0)
    edge_corners(f2, corn_out_b, 0)
    for shift in halo_b:
        shift.start()
    step_one(24, 16, SEG, cols - 2 * SEG)

    def build_two(r, _):
        shifted_row(a2, r + 1, f2[r], 0)
        return 0

    lax.fori_loop(0, rows, build_two, 0, unroll=2)

    def patch(a_ref, side_in, parts):
        def eight(i, _):
            base = pl.multiple_of(i * 8, 8)
            left, right = side_in[0, pl.ds(base, 8), :], side_in[1, pl.ds(base, 8), :]
            for k in range(8):
                for low, high, lane in parts:
                    patch_row(a_ref, base + k + 1, left[k : k + 1, low:high], right[k : k + 1, low:high], lane)
            return 0

        lax.fori_loop(0, rows // 8, eight, 0)

    def outer(a_ref, rows_in, corners, low, lane):
        high = low + rows_in.shape[2]
        for end, row in ((0, 0), (1, rows + 1)):
            shifted_row(a_ref, row, rows_in[end], lane)
            patch_row(a_ref, row, corners[2 * end, :, low:high], corners[2 * end + 1, :, low:high], lane)

    for shift in halo_a:
        shift.wait_recv()
    edge[...] = cols_in[...].astype(F32)
    patch(a1, edge, ((0, latent, 0), (latent, latent + width, split)))
    outer(a1, rows_a, corn_in, 0, 0)
    outer(a1, rows_h, corn_in, latent, split)

    step_one(0, 8, 0, cols)
    step_one(rows - 8, 8, 0, cols)
    step_one(8, 32, 0, SEG)
    step_one(8, 32, cols - SEG, SEG)
    edge_columns(h1, cols_out_1, edge_1, 0)
    edge_corners(h1, corn_out_1, 0)
    for shift in halo_1:
        shift.start()
    for shift in halo_b:
        shift.wait_recv()
    edge_b[...] = cols_in_b[...].astype(F32)
    patch(a2, edge_b, ((0, latent, 0),))
    outer(a2, rows_b, corn_in_b, 0, 0)

    def build_three(r, _):
        shifted_row(a2, r + 1, h1[r], split)
        return 0

    lax.fori_loop(0, rows, build_three, 0, unroll=2)
    early = part.shape[0]
    for s in range(early):
        part[s] = (
            jnp.dot(window(a2, s * step, step, 0, cols, 0, split), rows_of(w_f), preferred_element_type=F32) + bias
        )
    for shift in halo_1:
        shift.wait_recv()
    edge_1[...] = cols_in_1[...].astype(F32)
    patch(a2, edge_1, ((0, width, split),))
    outer(a2, rows_1, corn_in_1, 0, split)

    quarters = cols // SEG
    sent = step * quarters

    def forward(c, j, device):
        return pltpu.make_async_remote_copy(
            src_ref=normed.at[c * count + j],
            dst_ref=tok.at[c, me],
            send_sem=to_send,
            recv_sem=to_recv.at[c],
            device_id=device,
            device_id_type=MESH,
        )

    def send_forward(s):
        c, low = s * sent // count, s * sent % count // sent
        for j, device in torus.half(low):
            forward(c, j, device).start()

    def send_last(s):
        c, low = s * sent // count, s * sent % count // sent

        @pl.when(torus.low != low)
        def _():
            forward(c, *torus.mine(low)).start()

    def step_two(s):
        row = s * step
        cells = step * cols
        if s < early:
            hidden_taps = window(a2, row, step, 0, cols, split, a2.shape[2])
            gates = part[s] + jnp.dot(hidden_taps, rows_of(w_h), preferred_element_type=F32)
        else:
            gates = gates_of(a2, w, row, step, 0, cols, split) + bias
        new_cell, hid = lstm(gates, cl[pl.ds(row, step)].reshape(cells, width))
        cl[pl.ds(row, step)] = new_cell.reshape(step, cols, width)
        hid = hid.astype(BF)
        h2[pl.ds(row * quarters, sent)] = hid.reshape(sent, SEG, width)
        normed[pl.ds(row * quarters, sent)] = layer_norm(hid.astype(F32)).astype(BF).reshape(sent, SEG, width)
        pltpu.make_async_copy(cl.at[pl.ds(row, step)], cell_out.at[pl.ds(row, step)], out_sem.at[0]).start()

    for s in range(groups):
        if s:
            send_last(s - 1)
            send_forward(s - 1)
        step_two(s)
    for copy in late_loads:
        copy.wait()
    heads, blocks = head_mask()
    chunks = tok.shape[0]

    def wait_for(ref, sem):
        pltpu.make_async_remote_copy(
            src_ref=ref, dst_ref=ref, send_sem=to_send, recv_sem=sem, device_id=torus.here, device_id_type=MESH
        ).wait_recv()

    def send_back(c):
        for m, device in torus.others():
            pltpu.make_async_remote_copy(
                src_ref=ret.at[c, m],
                dst_ref=land.at[c * count + me],
                send_sem=back_send,
                recv_sem=back_recv.at[c],
                device_id=device,
                device_id_type=MESH,
            ).start()

    for c in range(chunks):
        tok[c, me] = normed[c * count + me]
        if c == 0:
            send_last(groups - 1)
        wait_for(tok.at[c, pl.ds(0, count - 1)], to_recv.at[c])
        if c == 0:
            send_forward(groups - 1)
        else:
            send_back(c - 1)
        attend_chunk(tok[c], w_qkv, w_out, heads, blocks, wide, qkv, prob, outs)
        for m in range(count):
            ret[c, m] = wide[pl.ds(m, SEG, stride=PITCH), :].astype(BF)
        land[c * count + me] = ret[c, me]
    send_back(chunks - 1)
    for c in range(chunks):
        base = c * count
        wait_for(land.at[pl.ds(base, count - 1)], back_recv.at[c])
        cells = count * SEG
        result = mlp_rows(
            h2[pl.ds(base, count)].reshape(cells, width), land[pl.ds(base, count)].reshape(cells, width), w_up, w_down
        )
        outb[pl.ds(c * SEG, SEG)] = result.reshape(SEG, cols, width)
        pltpu.make_async_copy(outb.at[pl.ds(c * SEG, SEG)], block_out.at[pl.ds(c * SEG, SEG)], out_sem.at[1]).start()
    for shift in halo_a + halo_b + halo_1:
        shift.wait_send()
    for sem, source in ((to_send, tok), (back_send, ret)):
        most = source.at[:, pl.ds(0, count - 1)]
        pltpu.make_async_remote_copy(
            src_ref=most, dst_ref=most, send_sem=sem, recv_sem=to_recv.at[0],
            device_id=torus.here, device_id_type=MESH,
        ).wait_send()
    pltpu.make_async_copy(cl, cell_out, out_sem.at[0]).wait()
    pltpu.make_async_copy(outb, block_out, out_sem.at[1]).wait()


def body(frames, hidden_state, cell_state, w_gates, gate_bias, w_qkv, w_out, w_up, w_down):
    rows, cols, width = hidden_state.shape
    latent = frames.shape[2] // 2
    gates = w_gates.shape[3]
    depth = 3 * (latent + width)
    members = lax.axis_size("gy") // 2 * lax.axis_size("gx")
    chunks = rows * cols // (members * SEG)
    cells = members * SEG
    any_space = pl.BlockSpec(memory_space=pl.ANY)
    dma = pltpu.SemaphoreType.DMA

    def vm(*shape, dtype=BF):
        return pltpu.VMEM(shape, dtype)

    def sides(span):
        return [
            vm(2, rows, span), vm(2, rows, span), vm(4, 1, span, dtype=F32), vm(4, 1, span, dtype=F32),
            vm(2, rows, span, dtype=F32),
        ]

    scratch = [
        vm(rows, cols, latent), vm(rows, cols, latent), vm(rows, cols, width), vm(rows, cols, width, dtype=F32),
        vm(3, 3, latent, gates), vm(3, 3, width, gates), vm(1, gates, dtype=F32), vm(*w_qkv.shape), vm(*w_out.shape), vm(*w_up.shape),
        vm(*w_down.shape),
        vm(rows + 2, cols, depth), vm(rows + 2, cols, depth), vm(rows, cols, width),
        vm(chunks * members, SEG, width), vm(chunks * members, SEG, width),
        vm(chunks, members, SEG, width), vm(chunks, members, SEG, width),
        vm(chunks * members, SEG, width), vm(rows, cols, width),
        vm(2, cols, latent), vm(2, cols, width), *sides(latent + width),
        vm(2, cols, latent), *sides(latent),
        vm(2, cols, width), *sides(width),
        vm(2, 8 * cols, gates, dtype=F32),
        vm(SEG * PITCH, width, dtype=F32), vm(cells, 3 * HEADS * HDIM), vm(2, cells, 256), vm(cells, HEADS * HDIM),
        dma((64,)), dma((10,)), dma((10,)), dma((8,)), dma((8,)), dma((8,)), dma((8,)),
        dma, dma((chunks,)), dma, dma((chunks,)), dma((2,)),
    ]
    return pl.pallas_call(
        kernel,
        out_shape=(jax.ShapeDtypeStruct(hidden_state.shape, BF), jax.ShapeDtypeStruct(cell_state.shape, F32)),
        in_specs=[any_space] * 9,
        out_specs=[any_space] * 2,
        scratch_shapes=scratch,
        compiler_params=pltpu.CompilerParams(vmem_limit_bytes=60 * 2**20, collective_id=1, has_side_effects=True),
        name="fused",
    )(frames, hidden_state, cell_state, w_gates, gate_bias[None], w_qkv, w_out, w_up, w_down)


def solution(mesh):
    spec = P("gy", "gx", None)
    return jax.shard_map(
        body,
        mesh=mesh,
        in_specs=(spec, spec, spec, P(), P(), P(), P(), P(), P()),
        out_specs=(spec, spec),
        check_vma=False,
    )
```

```python
import jax
import jax.numpy as jnp
from jax import lax
from jax.experimental import pallas as pl
from jax.experimental.pallas import tpu as pltpu
from jax.sharding import PartitionSpec as P

HEADS = 8
HDIM = 32
GRID = 8
SEG = 16
PITCH = 72
SIDE = 4
MESH = pl.DeviceIdType.MESH
BF = jnp.bfloat16
F32 = jnp.float32


def sigmoid(t):
    return 0.5 * jnp.tanh(0.5 * t) + 0.5


def layer_norm(values):
    center = values - jnp.mean(values, axis=-1, keepdims=True)
    spread = jnp.mean(center * center, axis=-1, keepdims=True)
    return center * lax.rsqrt(spread + 1e-05)


def shifted_row(a_ref, row, cells, lane):
    count, width = cells.shape
    wide = cells.astype(F32)
    a_ref[row, :, lane : lane + width] = pltpu.roll(wide, 1, 0).astype(BF)
    a_ref[row, :, lane + width : lane + 2 * width] = cells
    a_ref[row, :, lane + 2 * width : lane + 3 * width] = pltpu.roll(wide, count - 1, 0).astype(BF)


def patch_row(a_ref, row, left, right, lane):
    cols, width = a_ref.shape[1], left.shape[1]
    pos = lax.broadcasted_iota(jnp.int32, (SEG, width), 0)
    tile = a_ref[row, 0:SEG, lane : lane + width].astype(F32)
    a_ref[row, 0:SEG, lane : lane + width] = jnp.where(pos == 0, left, tile).astype(BF)
    lane += 2 * width
    tile = a_ref[row, cols - SEG : cols, lane : lane + width].astype(F32)
    a_ref[row, cols - SEG : cols, lane : lane + width] = jnp.where(pos == SEG - 1, right, tile).astype(BF)


def window(a_ref, row, rows, col, cols, low, high):
    taps = [a_ref[pl.ds(row + a, rows), col : col + cols, low:high].reshape(rows * cols, high - low) for a in range(3)]
    return jnp.concatenate(taps, axis=1)


def rows_of(w_ref):
    return w_ref[...].reshape(-1, w_ref.shape[3])


def whole(w_refs):
    return jnp.concatenate([rows_of(w) for w in w_refs], axis=0)


def gates_of(a_ref, w_ref, row, rows, col, cols, split):
    depth = a_ref.shape[2]
    taps = jnp.concatenate(
        [window(a_ref, row, rows, col, cols, 0, split), window(a_ref, row, rows, col, cols, split, depth)], axis=1
    )
    return jnp.dot(taps, whole(w_ref), preferred_element_type=F32)


def lstm(gates, cell):
    width = cell.shape[1]
    new_cell = sigmoid(gates[:, width : 2 * width]) * cell + sigmoid(gates[:, :width]) * jnp.tanh(
        gates[:, 2 * width : 3 * width]
    )
    return new_cell, sigmoid(gates[:, 3 * width :]) * jnp.tanh(new_cell)


def far_first(steps):
    return sorted(steps, key=lambda d: (-sum(min(v, SIDE - v) for v in d), sum(d) % 3, d))


class Torus:
    def __init__(self):
        gy, gx = lax.axis_index("gy"), lax.axis_index("gx")
        self.here = {"gy": gy, "gx": gx}
        self.parity = gy % 2
        k = gy // 2
        low, high, x, y = k // SIDE, gx % 2, gx // 2, k % SIDE
        self.low = low
        self.xs = [(x + d) % SIDE * 2 for d in range(SIDE)]
        self.ys = [(y + d) % SIDE for d in range(SIDE)]
        z = high * 2 + low
        self.zs = [((z + d) % SIDE % 2 * SIDE, (z + d) % SIDE // 2) for d in range(SIDE)]
        self.highs = [high, (high + 1) % 2]
        self.me = k * 2 * SIDE + gx

    def at(self, k, gx):
        return k * 2 * SIDE + gx, {"gy": 2 * k + self.parity, "gx": gx}

    def others(self):
        steps = [(a, b, c) for a in range(SIDE) for b in range(SIDE) for c in range(SIDE) if a or b or c]
        for a, b, c in far_first(steps):
            yield self.at(self.zs[c][0] + self.ys[b], self.xs[a] + self.zs[c][1])

    def half(self, low):
        steps = [(a, b, 2 * c) for a in range(SIDE) for b in range(SIDE) for c in range(2) if a or b or c]
        for a, b, c in far_first(steps):
            yield self.at(low * SIDE + self.ys[b], self.xs[a] + self.highs[c // 2])

    def mine(self, low):
        return self.at(low * SIDE + self.ys[0], self.xs[0] + self.highs[0])


class Shift:
    def __init__(self, src, dst, dy, dx, send_sem, recv_sem):
        gy, gx = lax.axis_index("gy"), lax.axis_index("gx")
        ny, nx = lax.axis_size("gy"), lax.axis_size("gx")

        def inside(y, x):
            return jnp.logical_and(jnp.logical_and(y >= 0, y < ny), jnp.logical_and(x >= 0, x < nx))

        self.dst = dst
        self.to = inside(gy + dy, gx + dx)
        self.come = inside(gy - dy, gx - dx)
        self.copy = pltpu.make_async_remote_copy(
            src_ref=src,
            dst_ref=dst,
            send_sem=send_sem,
            recv_sem=recv_sem,
            device_id={"gy": gy + dy, "gx": gx + dx},
            device_id_type=MESH,
        )

    def clear(self):
        @pl.when(jnp.logical_not(self.come))
        def _():
            self.dst[...] = jnp.zeros(self.dst.shape, self.dst.dtype)

    def start(self):
        @pl.when(self.to)
        def _():
            self.copy.start()

    def wait_recv(self):
        @pl.when(self.come)
        def _():
            self.copy.wait_recv()

    def wait_send(self):
        @pl.when(self.to)
        def _():
            self.copy.wait_send()


def shifts(pieces, cols_out, cols_in, corners_out, corners_in, send_sems, recv_sems):
    plan = []

    def add(src, dst, dy, dx):
        at = len(plan)
        plan.append(Shift(src, dst, dy, dx, send_sems.at[at], recv_sems.at[at]))

    for side, dx in ((1, -1), (0, 1)):
        add(cols_out.at[1 - side], cols_in.at[side], 0, dx)
    for dy, low in ((-1, 2), (1, 0)):
        for dx, side in ((-1, 1), (1, 0)):
            add(corners_out.at[3 - low - side], corners_in.at[low + side], dy, dx)
    for cells, rows_in in pieces:
        rows = cells.shape[0]
        add(cells.at[0], rows_in.at[1], -1, 0)
        add(cells.at[rows - 1], rows_in.at[0], 1, 0)
    return plan


def edge_columns(cells, cols_out, scratch, lane):
    rows, cols, width = cells.shape

    def eight(i, _):
        base = pl.multiple_of(i * 8, 8)
        low = [cells[base + k, 0:SEG, :].astype(F32)[0:1] for k in range(8)]
        high = [cells[base + k, cols - SEG : cols, :].astype(F32)[SEG - 1 : SEG] for k in range(8)]
        scratch[0, pl.ds(base, 8), lane : lane + width] = jnp.concatenate(low, axis=0)
        scratch[1, pl.ds(base, 8), lane : lane + width] = jnp.concatenate(high, axis=0)
        return 0

    lax.fori_loop(0, rows // 8, eight, 0)
    cols_out[:, :, lane : lane + width] = scratch[:, 0:rows, lane : lane + width].astype(BF)


def edge_corners(cells, corners_out, lane):
    rows, cols, width = cells.shape
    for k in range(4):
        row = (k // 2) * (rows - 1)
        if k % 2:
            cell = cells[row, cols - SEG : cols, :].astype(F32)[SEG - 1 : SEG]
        else:
            cell = cells[row, 0:SEG, :].astype(F32)[0:1]
        corners_out[k, :, lane : lane + width] = cell


def head_mask():
    row = lax.broadcasted_iota(jnp.int32, (256, 256), 0)
    col = lax.broadcasted_iota(jnp.int32, (256, 256), 1)
    heads = ((col % 128) // HDIM == row // 64).astype(F32).astype(BF)
    blocks = (col // 64 == row // 64).astype(F32).astype(BF)
    return heads, blocks


def attend_chunk(tokens, w_qkv, w_out, heads, blocks, wide, qkv, prob, outs):
    members = tokens.shape[0]
    cells = members * SEG
    wide[0:cells, :] = tokens.reshape(cells, 128).astype(F32)
    grouped = jnp.concatenate([wide[pl.ds(g, members, stride=SEG), :] for g in range(SEG)], axis=0).astype(BF)
    qkv[...] = jnp.dot(grouped, w_qkv[...], preferred_element_type=F32).astype(BF)
    zero = jnp.zeros((64, 128), BF)

    def spread(base, lane):
        pair = jnp.concatenate([qkv[base : base + 64, lane : lane + 128], qkv[base + 64 : base + 128, lane : lane + 128]], axis=1)
        return jnp.concatenate([pair] * 4, axis=0) * heads

    for base in range(0, cells, 128):
        for half in range(2):
            lane = half * 128
            q1 = jnp.concatenate([qkv[base : base + 64, lane : lane + 128], zero], axis=1)
            q2 = jnp.concatenate([zero, qkv[base + 64 : base + 128, lane : lane + 128]], axis=1)
            s = lax.dot_general(
                jnp.concatenate([q1, q2], axis=0),
                spread(base, 256 + lane),
                (((1,), (1,)), ((), ())),
                preferred_element_type=F32,
            )
            prob[half, base : base + 128, :] = jnp.minimum(jnp.exp(s * HDIM**-0.5), 3.3895e38).astype(BF)
    step = 512
    for base in range(0, cells, step):
        for half in range(2):
            raised = prob[half, base : base + step, :]
            total = jnp.dot(raised, blocks, preferred_element_type=F32)
            prob[half, base : base + step, :] = (raised.astype(F32) * (1.0 / total)).astype(BF)
    for base in range(0, cells, 128):
        for half in range(2):
            lane = half * 128
            o = jnp.dot(prob[half, base : base + 128, :], spread(base, 512 + lane), preferred_element_type=F32)
            outs[base : base + 64, lane : lane + 128] = o[:64, :128].astype(BF)
            outs[base + 64 : base + 128, lane : lane + 128] = o[64:, 128:].astype(BF)
    done = jnp.dot(outs[...], w_out[...], preferred_element_type=F32)
    for g in range(SEG):
        wide[g * PITCH : g * PITCH + members, :] = done[g * members : (g + 1) * members]


def mlp_rows(hidden, attended, w_up, w_down):
    mixed = hidden.astype(F32) + attended.astype(F32)
    normed = layer_norm(mixed).astype(BF)
    u = jnp.dot(normed, w_up[...], preferred_element_type=F32)
    twice = u + u * jnp.tanh(u * (0.7978845608 + 0.7978845608 * 0.044715 * (u * u)))
    return (mixed + 0.5 * jnp.dot(twice.astype(BF), w_down[...], preferred_element_type=F32)).astype(BF)


def kernel(*refs):
    names = iter(refs)
    take = lambda n: [next(names) for _ in range(n)]
    frames, hidden, cell, w_gates, bias_in, wqkv_in, wout_in, wup_in, wdown_in = take(9)
    outb, cl = take(2)
    f1, f2, hd, w_f, w_h, bias_v, w_qkv, w_out, w_up, w_down = take(10)
    w = (w_f, w_h)
    a1, a2, h1, h2, normed, tok, ret, land = take(8)
    rows_a, rows_h, cols_out, cols_in, corn_out, corn_in, edge = take(7)
    rows_b, cols_out_b, cols_in_b, corn_out_b, corn_in_b, edge_b = take(6)
    rows_1, cols_out_1, cols_in_1, corn_out_1, corn_in_1, edge_1 = take(6)
    part, wide, qkv, prob, outs = take(5)
    load_sem, send_a, recv_a, send_b, recv_b, send_1, recv_1, to_send, to_recv, back_send, back_recv = take(11)

    rows, cols, width = hd.shape
    latent = f1.shape[2]
    torus = Torus()
    gy, gx = torus.here["gy"], torus.here["gx"]
    ny, nx = lax.axis_size("gy"), lax.axis_size("gx")
    count = ny // 2 * nx
    me = torus.me
    split = 3 * latent
    step = 8
    groups = rows // step

    used = iter(range(64))

    def load(src, dst):
        return pltpu.make_async_copy(src, dst, load_sem.at[next(used)])

    first_loads = []
    bunch = 2 * step
    for row in range(0, rows, bunch):
        at = pl.ds(row, bunch)
        first_loads.append((load(frames.at[at, :, pl.ds(0, latent)], f1.at[at]), load(hidden.at[at], hd.at[at])))
    gate_loads = [
        load(w_gates.at[:, :, pl.ds(0, latent)], w_f),
        load(w_gates.at[:, :, pl.ds(latent, width)], w_h),
        load(cell, cl),
        load(bias_in, bias_v),
    ]
    load_f2 = load(frames.at[:, :, pl.ds(latent, latent)], f2)
    late_loads = [load(wqkv_in, w_qkv), load(wout_in, w_out), load(wup_in, w_up), load(wdown_in, w_down)]

    halo_a = shifts(((f1, rows_a), (hd, rows_h)), cols_out, cols_in, corn_out, corn_in, send_a, recv_a)
    halo_b = shifts(((f2, rows_b),), cols_out_b, cols_in_b, corn_out_b, corn_in_b, send_b, recv_b)
    halo_1 = shifts(((h1, rows_1),), cols_out_1, cols_in_1, corn_out_1, corn_in_1, send_1, recv_1)

    for pair in first_loads:
        for copy in pair:
            copy.start()
    barrier = pltpu.get_barrier_semaphore()

    for _, device in torus.others():
        pl.semaphore_signal(barrier, inc=1, device_id=device, device_id_type=MESH)
    greeted = count - 1
    for dy in (-1, 1):
        for dx in (-1, 0, 1):
            y, x = gy + dy, gx + dx
            near = jnp.logical_and(jnp.logical_and(y >= 0, y < ny), jnp.logical_and(x >= 0, x < nx))

            @pl.when(near)
            def _():
                pl.semaphore_signal(barrier, inc=1, device_id={"gy": y, "gx": x}, device_id_type=MESH)

            greeted = greeted + near.astype(jnp.int32)
    for copy in gate_loads + [load_f2] + late_loads:
        copy.start()
    for shift in halo_a + halo_b + halo_1:
        shift.clear()

    for g, pair in enumerate(first_loads):
        for copy in pair:
            copy.wait()

        def build(r, _):
            shifted_row(a1, r + 1, f1[r], 0)
            shifted_row(a1, r + 1, hd[r], split)
            return 0

        lax.fori_loop(g * bunch, g * bunch + bunch, build, 0, unroll=2)
    edge_columns(f1, cols_out, edge, 0)
    edge_columns(hd, cols_out, edge, latent)
    edge_corners(f1, corn_out, 0)
    edge_corners(hd, corn_out, latent)
    pl.semaphore_wait(barrier, greeted)
    for shift in halo_a:
        shift.start()
    for copy in gate_loads:
        copy.wait()
    bias = bias_v[...]

    def step_one(row, count_r, col, count_c):
        cells = count_r * count_c
        old = cl[pl.ds(row, count_r), col : col + count_c, :].reshape(cells, width)
        new_cell, hid = lstm(gates_of(a1, w, row, count_r, col, count_c, split) + bias, old)
        cl[pl.ds(row, count_r), col : col + count_c, :] = new_cell.reshape(count_r, count_c, width)
        h1[pl.ds(row, count_r), col : col + count_c, :] = hid.astype(BF).reshape(count_r, count_c, width)

    step_one(8, 16, SEG, cols - 2 * SEG)
    load_f2.wait()
    edge_columns(f2, cols_out_b, edge_b, 0)
    edge_corners(f2, corn_out_b, 0)
    for shift in halo_b:
        shift.start()
    step_one(24, 16, SEG, cols - 2 * SEG)

    def build_two(r, _):
        shifted_row(a2, r + 1, f2[r], 0)
        return 0

    lax.fori_loop(0, rows, build_two, 0, unroll=2)

    def patch(a_ref, side_in, parts):
        def eight(i, _):
            base = pl.multiple_of(i * 8, 8)
            left, right = side_in[0, pl.ds(base, 8), :], side_in[1, pl.ds(base, 8), :]
            for k in range(8):
                for low, high, lane in parts:
                    patch_row(a_ref, base + k + 1, left[k : k + 1, low:high], right[k : k + 1, low:high], lane)
            return 0

        lax.fori_loop(0, rows // 8, eight, 0)

    def outer(a_ref, rows_in, corners, low, lane):
        high = low + rows_in.shape[2]
        for end, row in ((0, 0), (1, rows + 1)):
            shifted_row(a_ref, row, rows_in[end], lane)
            patch_row(a_ref, row, corners[2 * end, :, low:high], corners[2 * end + 1, :, low:high], lane)

    for shift in halo_a:
        shift.wait_recv()
    edge[...] = cols_in[...].astype(F32)
    patch(a1, edge, ((0, latent, 0), (latent, latent + width, split)))
    outer(a1, rows_a, corn_in, 0, 0)
    outer(a1, rows_h, corn_in, latent, split)

    step_one(0, 8, 0, cols)
    step_one(rows - 8, 8, 0, cols)
    step_one(8, 32, 0, SEG)
    step_one(8, 32, cols - SEG, SEG)
    edge_columns(h1, cols_out_1, edge_1, 0)
    edge_corners(h1, corn_out_1, 0)
    for shift in halo_1:
        shift.start()
    for shift in halo_b:
        shift.wait_recv()
    edge_b[...] = cols_in_b[...].astype(F32)
    patch(a2, edge_b, ((0, latent, 0),))
    outer(a2, rows_b, corn_in_b, 0, 0)

    def build_three(r, _):
        shifted_row(a2, r + 1, h1[r], split)
        return 0

    lax.fori_loop(0, rows, build_three, 0, unroll=2)
    early = part.shape[0]
    for s in range(early):
        part[s] = (
            jnp.dot(window(a2, s * step, step, 0, cols, 0, split), rows_of(w_f), preferred_element_type=F32) + bias
        )
    for shift in halo_1:
        shift.wait_recv()
    edge_1[...] = cols_in_1[...].astype(F32)
    patch(a2, edge_1, ((0, width, split),))
    outer(a2, rows_1, corn_in_1, 0, split)

    quarters = cols // SEG
    sent = step * quarters

    def forward(c, j, device):
        return pltpu.make_async_remote_copy(
            src_ref=normed.at[c * count + j],
            dst_ref=tok.at[c, me],
            send_sem=to_send,
            recv_sem=to_recv.at[c],
            device_id=device,
            device_id_type=MESH,
        )

    def send_forward(s):
        c, low = s * sent // count, s * sent % count // sent
        for j, device in torus.half(low):
            forward(c, j, device).start()

    def send_last(s):
        c, low = s * sent // count, s * sent % count // sent

        @pl.when(torus.low != low)
        def _():
            forward(c, *torus.mine(low)).start()

    def step_two(s):
        row = s * step
        cells = step * cols
        if s < early:
            hidden_taps = window(a2, row, step, 0, cols, split, a2.shape[2])
            gates = part[s] + jnp.dot(hidden_taps, rows_of(w_h), preferred_element_type=F32)
        else:
            gates = gates_of(a2, w, row, step, 0, cols, split) + bias
        new_cell, hid = lstm(gates, cl[pl.ds(row, step)].reshape(cells, width))
        cl[pl.ds(row, step)] = new_cell.reshape(step, cols, width)
        hid = hid.astype(BF)
        h2[pl.ds(row * quarters, sent)] = hid.reshape(sent, SEG, width)
        normed[pl.ds(row * quarters, sent)] = layer_norm(hid.astype(F32)).astype(BF).reshape(sent, SEG, width)

    for s in range(groups):
        if s:
            send_last(s - 1)
            send_forward(s - 1)
        step_two(s)
    for copy in late_loads:
        copy.wait()
    heads, blocks = head_mask()
    chunks = tok.shape[0]

    def wait_for(ref, sem):
        pltpu.make_async_remote_copy(
            src_ref=ref, dst_ref=ref, send_sem=to_send, recv_sem=sem, device_id=torus.here, device_id_type=MESH
        ).wait_recv()

    def send_back(c):
        for m, device in torus.others():
            pltpu.make_async_remote_copy(
                src_ref=ret.at[c, m],
                dst_ref=land.at[c * count + me],
                send_sem=back_send,
                recv_sem=back_recv.at[c],
                device_id=device,
                device_id_type=MESH,
            ).start()

    for c in range(chunks):
        tok[c, me] = normed[c * count + me]
        if c == 0:
            send_last(groups - 1)
        wait_for(tok.at[c, pl.ds(0, count - 1)], to_recv.at[c])
        if c == 0:
            send_forward(groups - 1)
        else:
            send_back(c - 1)
        attend_chunk(tok[c], w_qkv, w_out, heads, blocks, wide, qkv, prob, outs)
        for m in range(count):
            ret[c, m] = wide[pl.ds(m, SEG, stride=PITCH), :].astype(BF)
        land[c * count + me] = ret[c, me]
    send_back(chunks - 1)
    for c in range(chunks):
        base = c * count
        wait_for(land.at[pl.ds(base, count - 1)], back_recv.at[c])
        cells = count * SEG
        result = mlp_rows(
            h2[pl.ds(base, count)].reshape(cells, width), land[pl.ds(base, count)].reshape(cells, width), w_up, w_down
        )
        outb[pl.ds(c * SEG, SEG)] = result.reshape(SEG, cols, width)
    for shift in halo_a + halo_b + halo_1:
        shift.wait_send()
    for sem, source in ((to_send, tok), (back_send, ret)):
        most = source.at[:, pl.ds(0, count - 1)]
        pltpu.make_async_remote_copy(
            src_ref=most, dst_ref=most, send_sem=sem, recv_sem=to_recv.at[0],
            device_id=torus.here, device_id_type=MESH,
        ).wait_send()


def body(frames, hidden_state, cell_state, w_gates, gate_bias, w_qkv, w_out, w_up, w_down):
    rows, cols, width = hidden_state.shape
    latent = frames.shape[2] // 2
    gates = w_gates.shape[3]
    depth = 3 * (latent + width)
    members = lax.axis_size("gy") // 2 * lax.axis_size("gx")
    chunks = rows * cols // (members * SEG)
    cells = members * SEG
    any_space = pl.BlockSpec(memory_space=pl.ANY)
    dma = pltpu.SemaphoreType.DMA

    def vm(*shape, dtype=BF):
        return pltpu.VMEM(shape, dtype)

    def sides(span):
        return [
            vm(2, rows, span), vm(2, rows, span), vm(4, 1, span, dtype=F32), vm(4, 1, span, dtype=F32),
            vm(2, rows, span, dtype=F32),
        ]

    scratch = [
        vm(rows, cols, latent), vm(rows, cols, latent), vm(rows, cols, width),
        vm(3, 3, latent, gates), vm(3, 3, width, gates), vm(1, gates, dtype=F32), vm(*w_qkv.shape), vm(*w_out.shape), vm(*w_up.shape),
        vm(*w_down.shape),
        vm(rows + 2, cols, depth), vm(rows + 2, cols, depth), vm(rows, cols, width),
        vm(chunks * members, SEG, width), vm(chunks * members, SEG, width),
        vm(chunks, members, SEG, width), vm(chunks, members, SEG, width),
        vm(chunks * members, SEG, width),
        vm(2, cols, latent), vm(2, cols, width), *sides(latent + width),
        vm(2, cols, latent), *sides(latent),
        vm(2, cols, width), *sides(width),
        vm(2, 8 * cols, gates, dtype=F32),
        vm(SEG * PITCH, width, dtype=F32), vm(cells, 3 * HEADS * HDIM), vm(2, cells, 256), vm(cells, HEADS * HDIM),
        dma((64,)), dma((10,)), dma((10,)), dma((8,)), dma((8,)), dma((8,)), dma((8,)),
        dma, dma((chunks,)), dma, dma((chunks,)),
    ]
    return pl.pallas_call(
        kernel,
        out_shape=(pltpu.VMEM(hidden_state.shape, BF), pltpu.VMEM(cell_state.shape, F32)),
        in_specs=[any_space] * 9,
        out_specs=[pl.BlockSpec(memory_space=pltpu.VMEM)] * 2,
        scratch_shapes=scratch,
        compiler_params=pltpu.CompilerParams(vmem_limit_bytes=56 * 2**20, collective_id=1, has_side_effects=True),
        name="fused",
    )(frames, hidden_state, cell_state, w_gates, gate_bias[None], w_qkv, w_out, w_up, w_down)


def solution(mesh):
    spec = P("gy", "gx", None)
    return jax.shard_map(
        body,
        mesh=mesh,
        in_specs=(spec, spec, spec, P(), P(), P(), P(), P(), P()),
        out_specs=(spec, spec),
        check_vma=False,
    )
```

```python
import jax
import jax.numpy as jnp
from jax import lax
from jax.experimental import pallas as pl
from jax.experimental.pallas import tpu as pltpu
from jax.sharding import PartitionSpec as P

HEADS = 8
HDIM = 32
GRID = 8
SEG = 16
PITCH = 72
SIDE = 4
MESH = pl.DeviceIdType.MESH
BF = jnp.bfloat16
F32 = jnp.float32


def sigmoid(t):
    return 0.5 * jnp.tanh(0.5 * t) + 0.5


def layer_norm(values):
    center = values - jnp.mean(values, axis=-1, keepdims=True)
    spread = jnp.mean(center * center, axis=-1, keepdims=True)
    return center * lax.rsqrt(spread + 1e-05)


def shifted_row(a_ref, row, cells, lane):
    count, width = cells.shape
    wide = cells.astype(F32)
    a_ref[row, :, lane : lane + width] = pltpu.roll(wide, 1, 0).astype(BF)
    a_ref[row, :, lane + width : lane + 2 * width] = cells
    a_ref[row, :, lane + 2 * width : lane + 3 * width] = pltpu.roll(wide, count - 1, 0).astype(BF)


def patch_row(a_ref, row, left, right, lane):
    cols, width = a_ref.shape[1], left.shape[1]
    pos = lax.broadcasted_iota(jnp.int32, (SEG, width), 0)
    tile = a_ref[row, 0:SEG, lane : lane + width].astype(F32)
    a_ref[row, 0:SEG, lane : lane + width] = jnp.where(pos == 0, left, tile).astype(BF)
    lane += 2 * width
    tile = a_ref[row, cols - SEG : cols, lane : lane + width].astype(F32)
    a_ref[row, cols - SEG : cols, lane : lane + width] = jnp.where(pos == SEG - 1, right, tile).astype(BF)


def tap_rows(frame_taps, hidden_taps):
    return [v.reshape(-1, v.shape[-1]) for v in (frame_taps, hidden_taps)]


def mixed_taps(w_ref, mix_ref):
    cols, depth = w_ref.shape[1:3]
    step = 32

    def some(i, _):
        at = pl.ds(pl.multiple_of(i * step, step), step)
        for b in range(cols):
            ends = w_ref[0, b, at].astype(F32) + w_ref[2, b, at].astype(F32)
            middle = w_ref[1, b, at].astype(F32)
            mix_ref[0, b, at] = (0.5 * (ends + middle)).astype(BF)
            mix_ref[1, b, at] = (0.5 * (ends - middle)).astype(BF)
        return 0

    lax.fori_loop(0, depth // step, some, 0)


def conv_rows(a_ref, held, weights, row, rows, col, cols, low, high):
    x = [a_ref[row + i, col : col + cols, low:high] for i in range(rows + 2)]
    pairs = range(0, rows, 2)
    inputs = (
        [x[p] - x[p + 2] for p in pairs],
        [x[p + 1] + x[p + 2] for p in pairs],
        [x[p + 2] - x[p + 1] for p in pairs],
        [x[p + 1] - x[p + 3] for p in pairs],
    )
    m = [
        jnp.dot(jnp.concatenate(d, axis=0), g, preferred_element_type=F32) for d, g in zip(inputs, weights, strict=True)
    ]
    held[0], held[1] = m[1], m[2]
    even, odd = (held[0] + held[1]) + m[0], (held[0] - held[1]) - m[3]
    out = []
    for i in range(rows // 2):
        out += [even[i * cols : (i + 1) * cols], odd[i * cols : (i + 1) * cols]]
    return jnp.concatenate(out, axis=0)


def lstm(gates, cell):
    width = cell.shape[1]
    new_cell = sigmoid(gates[:, width : 2 * width]) * cell + sigmoid(gates[:, :width]) * jnp.tanh(
        gates[:, 2 * width : 3 * width]
    )
    return new_cell, sigmoid(gates[:, 3 * width :]) * jnp.tanh(new_cell)


def far_first(steps):
    return sorted(steps, key=lambda d: (-sum(min(v, SIDE - v) for v in d), sum(d) % 3, d))


class Torus:
    def __init__(self):
        gy, gx = lax.axis_index("gy"), lax.axis_index("gx")
        self.here = {"gy": gy, "gx": gx}
        self.parity = gy % 2
        k = gy // 2
        low, high, x, y = k // SIDE, gx % 2, gx // 2, k % SIDE
        self.low = low
        self.xs = [(x + d) % SIDE * 2 for d in range(SIDE)]
        self.ys = [(y + d) % SIDE for d in range(SIDE)]
        z = high * 2 + low
        self.zs = [((z + d) % SIDE % 2 * SIDE, (z + d) % SIDE // 2) for d in range(SIDE)]
        self.highs = [high, (high + 1) % 2]
        self.me = k * 2 * SIDE + gx

    def at(self, k, gx):
        return k * 2 * SIDE + gx, {"gy": 2 * k + self.parity, "gx": gx}

    def others(self):
        steps = [(a, b, c) for a in range(SIDE) for b in range(SIDE) for c in range(SIDE) if a or b or c]
        for a, b, c in far_first(steps):
            yield self.at(self.zs[c][0] + self.ys[b], self.xs[a] + self.zs[c][1])

    def half(self, low):
        steps = [(a, b, 2 * c) for a in range(SIDE) for b in range(SIDE) for c in range(2) if a or b or c]
        for a, b, c in far_first(steps):
            yield self.at(low * SIDE + self.ys[b], self.xs[a] + self.highs[c // 2])

    def mine(self, low):
        return self.at(low * SIDE + self.ys[0], self.xs[0] + self.highs[0])


class Shift:
    def __init__(self, src, dst, dy, dx, send_sem, recv_sem):
        gy, gx = lax.axis_index("gy"), lax.axis_index("gx")
        ny, nx = lax.axis_size("gy"), lax.axis_size("gx")

        def inside(y, x):
            return jnp.logical_and(jnp.logical_and(y >= 0, y < ny), jnp.logical_and(x >= 0, x < nx))

        self.dst = dst
        self.to = inside(gy + dy, gx + dx)
        self.come = inside(gy - dy, gx - dx)
        self.copy = pltpu.make_async_remote_copy(
            src_ref=src,
            dst_ref=dst,
            send_sem=send_sem,
            recv_sem=recv_sem,
            device_id={"gy": gy + dy, "gx": gx + dx},
            device_id_type=MESH,
        )

    def clear(self):
        @pl.when(jnp.logical_not(self.come))
        def _():
            self.dst[...] = jnp.zeros(self.dst.shape, self.dst.dtype)

    def start(self):
        @pl.when(self.to)
        def _():
            self.copy.start()

    def wait_recv(self):
        @pl.when(self.come)
        def _():
            self.copy.wait_recv()

    def wait_send(self):
        @pl.when(self.to)
        def _():
            self.copy.wait_send()


def shifts(pieces, cols_out, cols_in, corners_out, corners_in, send_sems, recv_sems):
    plan = []

    def add(src, dst, dy, dx):
        at = len(plan)
        plan.append(Shift(src, dst, dy, dx, send_sems.at[at], recv_sems.at[at]))

    for side, dx in ((1, -1), (0, 1)):
        add(cols_out.at[1 - side], cols_in.at[side], 0, dx)
    for dy, low in ((-1, 2), (1, 0)):
        for dx, side in ((-1, 1), (1, 0)):
            add(corners_out.at[3 - low - side], corners_in.at[low + side], dy, dx)
    for cells, rows_in in pieces:
        rows = cells.shape[0]
        add(cells.at[0], rows_in.at[1], -1, 0)
        add(cells.at[rows - 1], rows_in.at[0], 1, 0)
    return plan


def edge_columns(cells, cols_out, scratch, lane):
    rows, cols, width = cells.shape

    def eight(i, _):
        base = pl.multiple_of(i * 8, 8)
        low = [cells[base + k, 0:SEG, :].astype(F32)[0:1] for k in range(8)]
        high = [cells[base + k, cols - SEG : cols, :].astype(F32)[SEG - 1 : SEG] for k in range(8)]
        scratch[0, pl.ds(base, 8), lane : lane + width] = jnp.concatenate(low, axis=0)
        scratch[1, pl.ds(base, 8), lane : lane + width] = jnp.concatenate(high, axis=0)
        return 0

    lax.fori_loop(0, rows // 8, eight, 0)
    cols_out[:, :, lane : lane + width] = scratch[:, 0:rows, lane : lane + width].astype(BF)


def edge_corners(cells, corners_out, lane):
    rows, cols, width = cells.shape
    for k in range(4):
        row = (k // 2) * (rows - 1)
        if k % 2:
            cell = cells[row, cols - SEG : cols, :].astype(F32)[SEG - 1 : SEG]
        else:
            cell = cells[row, 0:SEG, :].astype(F32)[0:1]
        corners_out[k, :, lane : lane + width] = cell


def head_mask():
    row = lax.broadcasted_iota(jnp.int32, (256, 256), 0)
    col = lax.broadcasted_iota(jnp.int32, (256, 256), 1)
    heads = ((col % 128) // HDIM == row // 64).astype(F32).astype(BF)
    blocks = (col // 64 == row // 64).astype(F32).astype(BF)
    return heads, blocks


def attend_chunk(tokens, w_qkv, w_out, heads, blocks, wide, qkv, prob, outs):
    members = tokens.shape[0]
    cells = members * SEG
    wide[0:cells, :] = tokens.reshape(cells, 128).astype(F32)
    grouped = jnp.concatenate([wide[pl.ds(g, members, stride=SEG), :] for g in range(SEG)], axis=0).astype(BF)
    qkv[...] = jnp.dot(grouped, w_qkv[...], preferred_element_type=F32).astype(BF)
    zero = jnp.zeros((64, 128), BF)

    def spread(base, lane):
        pair = jnp.concatenate([qkv[base : base + 64, lane : lane + 128], qkv[base + 64 : base + 128, lane : lane + 128]], axis=1)
        return jnp.concatenate([pair] * 4, axis=0) * heads

    for base in range(0, cells, 128):
        for half in range(2):
            lane = half * 128
            q1 = jnp.concatenate([qkv[base : base + 64, lane : lane + 128], zero], axis=1)
            q2 = jnp.concatenate([zero, qkv[base + 64 : base + 128, lane : lane + 128]], axis=1)
            s = lax.dot_general(
                jnp.concatenate([q1, q2], axis=0),
                spread(base, 256 + lane),
                (((1,), (1,)), ((), ())),
                preferred_element_type=F32,
            )
            prob[half, base : base + 128, :] = jnp.minimum(jnp.exp(s * HDIM**-0.5), 3.3895e38).astype(BF)
    step = 512
    for base in range(0, cells, step):
        for half in range(2):
            raised = prob[half, base : base + step, :]
            total = jnp.dot(raised, blocks, preferred_element_type=F32)
            prob[half, base : base + step, :] = (raised.astype(F32) * (1.0 / total)).astype(BF)
    for base in range(0, cells, 128):
        for half in range(2):
            lane = half * 128
            o = jnp.dot(prob[half, base : base + 128, :], spread(base, 512 + lane), preferred_element_type=F32)
            outs[base : base + 64, lane : lane + 128] = o[:64, :128].astype(BF)
            outs[base + 64 : base + 128, lane : lane + 128] = o[64:, 128:].astype(BF)
    done = jnp.dot(outs[...], w_out[...], preferred_element_type=F32)
    for g in range(SEG):
        wide[g * PITCH : g * PITCH + members, :] = done[g * members : (g + 1) * members]


def mlp_rows(hidden, attended, w_up, w_down):
    mixed = hidden.astype(F32) + attended.astype(F32)
    normed = layer_norm(mixed).astype(BF)
    u = jnp.dot(normed, w_up[...], preferred_element_type=F32)
    twice = u + u * jnp.tanh(u * (0.7978845608 + 0.7978845608 * 0.044715 * (u * u)))
    return (mixed + 0.5 * jnp.dot(twice.astype(BF), w_down[...], preferred_element_type=F32)).astype(BF)


def kernel(*refs):
    names = iter(refs)
    take = lambda n: [next(names) for _ in range(n)]
    frames, hidden, cell, w_gates, bias_in, wqkv_in, wout_in, wup_in, wdown_in = take(9)
    outb, cl = take(2)
    f1, f2, hd, w_f, w_h, mix_f, mix_h, bias_v, w_qkv, w_out, w_up, w_down = take(12)
    a1, a2, h1, h2, normed, tok, ret, land = take(8)
    rows_a, rows_h, cols_out, cols_in, corn_out, corn_in, edge = take(7)
    rows_b, cols_out_b, cols_in_b, corn_out_b, corn_in_b, edge_b = take(6)
    rows_1, cols_out_1, cols_in_1, corn_out_1, corn_in_1, edge_1 = take(6)
    part, held, wide, qkv, prob, outs = take(6)
    load_sem, send_a, recv_a, send_b, recv_b, send_1, recv_1, to_send, to_recv, back_send, back_recv = take(11)

    rows, cols, width = hd.shape
    latent = f1.shape[2]
    torus = Torus()
    gy, gx = torus.here["gy"], torus.here["gx"]
    ny, nx = lax.axis_size("gy"), lax.axis_size("gx")
    count = ny // 2 * nx
    me = torus.me
    split = 3 * latent
    step = 8
    groups = rows // step

    used = iter(range(64))

    def load(src, dst):
        return pltpu.make_async_copy(src, dst, load_sem.at[next(used)])

    first_loads = []
    bunch = 2 * step
    for row in range(0, rows, bunch):
        at = pl.ds(row, bunch)
        first_loads.append((load(frames.at[at, :, pl.ds(0, latent)], f1.at[at]), load(hidden.at[at], hd.at[at])))
    gate_loads = [
        load(w_gates.at[:, :, pl.ds(0, latent)], w_f),
        load(w_gates.at[:, :, pl.ds(latent, width)], w_h),
        load(cell, cl),
        load(bias_in, bias_v),
    ]
    load_f2 = load(frames.at[:, :, pl.ds(latent, latent)], f2)
    late_loads = [load(wqkv_in, w_qkv), load(wout_in, w_out), load(wup_in, w_up), load(wdown_in, w_down)]

    halo_a = shifts(((f1, rows_a), (hd, rows_h)), cols_out, cols_in, corn_out, corn_in, send_a, recv_a)
    halo_b = shifts(((f2, rows_b),), cols_out_b, cols_in_b, corn_out_b, corn_in_b, send_b, recv_b)
    halo_1 = shifts(((h1, rows_1),), cols_out_1, cols_in_1, corn_out_1, corn_in_1, send_1, recv_1)

    for pair in first_loads:
        for copy in pair:
            copy.start()
    barrier = pltpu.get_barrier_semaphore()

    for _, device in torus.others():
        pl.semaphore_signal(barrier, inc=1, device_id=device, device_id_type=MESH)
    greeted = count - 1
    for dy in (-1, 1):
        for dx in (-1, 0, 1):
            y, x = gy + dy, gx + dx
            near = jnp.logical_and(jnp.logical_and(y >= 0, y < ny), jnp.logical_and(x >= 0, x < nx))

            @pl.when(near)
            def _():
                pl.semaphore_signal(barrier, inc=1, device_id={"gy": y, "gx": x}, device_id_type=MESH)

            greeted = greeted + near.astype(jnp.int32)
    for copy in gate_loads + [load_f2] + late_loads:
        copy.start()
    for shift in halo_a + halo_b + halo_1:
        shift.clear()

    for g, pair in enumerate(first_loads):
        for copy in pair:
            copy.wait()

        def build(r, _):
            shifted_row(a1, r + 1, f1[r], 0)
            shifted_row(a1, r + 1, hd[r], split)
            return 0

        lax.fori_loop(g * bunch, g * bunch + bunch, build, 0, unroll=2)
    edge_columns(f1, cols_out, edge, 0)
    edge_columns(hd, cols_out, edge, latent)
    edge_corners(f1, corn_out, 0)
    edge_corners(hd, corn_out, latent)
    pl.semaphore_wait(barrier, greeted)
    for shift in halo_a:
        shift.start()
    for copy in gate_loads:
        copy.wait()
    bias = bias_v[...]
    mixed_taps(w_f, mix_f)
    mixed_taps(w_h, mix_h)

    def frame_taps():
        return [tap_rows(f, h)[0] for f, h in four()]

    def hidden_taps():
        return [tap_rows(f, h)[1] for f, h in four()]

    def four():
        return [(w_f[0], w_h[0]), (mix_f[0], mix_h[0]), (mix_f[1], mix_h[1]), (w_f[2], w_h[2])]

    def both_taps():
        return [jnp.concatenate(tap_rows(f, h), axis=0) for f, h in four()]

    def gates_of(a_ref, row, rows, col, cols):
        return conv_rows(a_ref, held, both_taps(), row, rows, col, cols, 0, a_ref.shape[2]) + bias

    def step_one(row, count_r, col, count_c):
        cells = count_r * count_c
        old = cl[pl.ds(row, count_r), col : col + count_c, :].reshape(cells, width)
        new_cell, hid = lstm(gates_of(a1, row, count_r, col, count_c), old)
        cl[pl.ds(row, count_r), col : col + count_c, :] = new_cell.reshape(count_r, count_c, width)
        h1[pl.ds(row, count_r), col : col + count_c, :] = hid.astype(BF).reshape(count_r, count_c, width)

    step_one(8, 16, SEG, cols - 2 * SEG)
    load_f2.wait()
    edge_columns(f2, cols_out_b, edge_b, 0)
    edge_corners(f2, corn_out_b, 0)
    for shift in halo_b:
        shift.start()
    step_one(24, 16, SEG, cols - 2 * SEG)

    def build_two(r, _):
        shifted_row(a2, r + 1, f2[r], 0)
        return 0

    lax.fori_loop(0, rows, build_two, 0, unroll=2)

    def patch(a_ref, side_in, parts):
        def eight(i, _):
            base = pl.multiple_of(i * 8, 8)
            left, right = side_in[0, pl.ds(base, 8), :], side_in[1, pl.ds(base, 8), :]
            for k in range(8):
                for low, high, lane in parts:
                    patch_row(a_ref, base + k + 1, left[k : k + 1, low:high], right[k : k + 1, low:high], lane)
            return 0

        lax.fori_loop(0, rows // 8, eight, 0)

    def outer(a_ref, rows_in, corners, low, lane):
        high = low + rows_in.shape[2]
        for end, row in ((0, 0), (1, rows + 1)):
            shifted_row(a_ref, row, rows_in[end], lane)
            patch_row(a_ref, row, corners[2 * end, :, low:high], corners[2 * end + 1, :, low:high], lane)

    for shift in halo_a:
        shift.wait_recv()
    edge[...] = cols_in[...].astype(F32)
    patch(a1, edge, ((0, latent, 0), (latent, latent + width, split)))
    outer(a1, rows_a, corn_in, 0, 0)
    outer(a1, rows_h, corn_in, latent, split)

    step_one(0, 8, 0, cols)
    step_one(rows - 8, 8, 0, cols)
    step_one(8, 32, 0, SEG)
    step_one(8, 32, cols - SEG, SEG)
    edge_columns(h1, cols_out_1, edge_1, 0)
    edge_corners(h1, corn_out_1, 0)
    for shift in halo_1:
        shift.start()
    for shift in halo_b:
        shift.wait_recv()
    edge_b[...] = cols_in_b[...].astype(F32)
    patch(a2, edge_b, ((0, latent, 0),))
    outer(a2, rows_b, corn_in_b, 0, 0)

    def build_three(r, _):
        shifted_row(a2, r + 1, h1[r], split)
        return 0

    lax.fori_loop(0, rows, build_three, 0, unroll=2)
    early = part.shape[0]
    for s in range(early):
        part[s] = conv_rows(a2, held, frame_taps(), s * step, step, 0, cols, 0, split) + bias
    for shift in halo_1:
        shift.wait_recv()
    edge_1[...] = cols_in_1[...].astype(F32)
    patch(a2, edge_1, ((0, width, split),))
    outer(a2, rows_1, corn_in_1, 0, split)

    quarters = cols // SEG
    sent = step * quarters

    def forward(c, j, device):
        return pltpu.make_async_remote_copy(
            src_ref=normed.at[c * count + j],
            dst_ref=tok.at[c, me],
            send_sem=to_send,
            recv_sem=to_recv.at[c],
            device_id=device,
            device_id_type=MESH,
        )

    def send_forward(s):
        c, low = s * sent // count, s * sent % count // sent
        for j, device in torus.half(low):
            forward(c, j, device).start()

    def send_last(s):
        c, low = s * sent // count, s * sent % count // sent

        @pl.when(torus.low != low)
        def _():
            forward(c, *torus.mine(low)).start()

    def step_two(s):
        row = s * step
        cells = step * cols
        if s < early:
            gates = part[s] + conv_rows(a2, held, hidden_taps(), row, step, 0, cols, split, a2.shape[2])
        else:
            gates = gates_of(a2, row, step, 0, cols)
        new_cell, hid = lstm(gates, cl[pl.ds(row, step)].reshape(cells, width))
        cl[pl.ds(row, step)] = new_cell.reshape(step, cols, width)
        hid = hid.astype(BF)
        h2[pl.ds(row * quarters, sent)] = hid.reshape(sent, SEG, width)
        normed[pl.ds(row * quarters, sent)] = layer_norm(hid.astype(F32)).astype(BF).reshape(sent, SEG, width)

    for s in range(groups):
        if s:
            send_last(s - 1)
            send_forward(s - 1)
        step_two(s)
    for copy in late_loads:
        copy.wait()
    heads, blocks = head_mask()
    chunks = tok.shape[0]

    def wait_for(ref, sem):
        pltpu.make_async_remote_copy(
            src_ref=ref, dst_ref=ref, send_sem=to_send, recv_sem=sem, device_id=torus.here, device_id_type=MESH
        ).wait_recv()

    def send_back(c):
        for m, device in torus.others():
            pltpu.make_async_remote_copy(
                src_ref=ret.at[c, m],
                dst_ref=land.at[c * count + me],
                send_sem=back_send,
                recv_sem=back_recv.at[c],
                device_id=device,
                device_id_type=MESH,
            ).start()

    for c in range(chunks):
        tok[c, me] = normed[c * count + me]
        if c == 0:
            send_last(groups - 1)
        wait_for(tok.at[c, pl.ds(0, count - 1)], to_recv.at[c])
        if c == 0:
            send_forward(groups - 1)
        else:
            send_back(c - 1)
        attend_chunk(tok[c], w_qkv, w_out, heads, blocks, wide, qkv, prob, outs)
        for m in range(count):
            ret[c, m] = wide[pl.ds(m, SEG, stride=PITCH), :].astype(BF)
        land[c * count + me] = ret[c, me]
    send_back(chunks - 1)
    for c in range(chunks):
        base = c * count
        wait_for(land.at[pl.ds(base, count - 1)], back_recv.at[c])
        cells = count * SEG
        result = mlp_rows(
            h2[pl.ds(base, count)].reshape(cells, width), land[pl.ds(base, count)].reshape(cells, width), w_up, w_down
        )
        outb[pl.ds(c * SEG, SEG)] = result.reshape(SEG, cols, width)
    for shift in halo_a + halo_b + halo_1:
        shift.wait_send()
    for sem, source in ((to_send, tok), (back_send, ret)):
        most = source.at[:, pl.ds(0, count - 1)]
        pltpu.make_async_remote_copy(
            src_ref=most, dst_ref=most, send_sem=sem, recv_sem=to_recv.at[0],
            device_id=torus.here, device_id_type=MESH,
        ).wait_send()


def body(frames, hidden_state, cell_state, w_gates, gate_bias, w_qkv, w_out, w_up, w_down):
    rows, cols, width = hidden_state.shape
    latent = frames.shape[2] // 2
    gates = w_gates.shape[3]
    depth = 3 * (latent + width)
    members = lax.axis_size("gy") // 2 * lax.axis_size("gx")
    chunks = rows * cols // (members * SEG)
    cells = members * SEG
    any_space = pl.BlockSpec(memory_space=pl.ANY)
    dma = pltpu.SemaphoreType.DMA

    def vm(*shape, dtype=BF):
        return pltpu.VMEM(shape, dtype)

    def sides(span):
        return [
            vm(2, rows, span), vm(2, rows, span), vm(4, 1, span, dtype=F32), vm(4, 1, span, dtype=F32),
            vm(2, rows, span, dtype=F32),
        ]

    scratch = [
        vm(rows, cols, latent), vm(rows, cols, latent), vm(rows, cols, width),
        vm(3, 3, latent, gates), vm(3, 3, width, gates), vm(2, 3, latent, gates), vm(2, 3, width, gates),
        vm(1, gates, dtype=F32), vm(*w_qkv.shape), vm(*w_out.shape), vm(*w_up.shape),
        vm(*w_down.shape),
        vm(rows + 2, cols, depth), vm(rows + 2, cols, depth), vm(rows, cols, width),
        vm(chunks * members, SEG, width), vm(chunks * members, SEG, width),
        vm(chunks, members, SEG, width), vm(chunks, members, SEG, width),
        vm(chunks * members, SEG, width),
        vm(2, cols, latent), vm(2, cols, width), *sides(latent + width),
        vm(2, cols, latent), *sides(latent),
        vm(2, cols, width), *sides(width),
        vm(3, 8 * cols, gates, dtype=F32), vm(2, 4 * cols, gates, dtype=F32),
        vm(SEG * PITCH, width, dtype=F32), vm(cells, 3 * HEADS * HDIM), vm(2, cells, 256), vm(cells, HEADS * HDIM),
        dma((64,)), dma((10,)), dma((10,)), dma((8,)), dma((8,)), dma((8,)), dma((8,)),
        dma, dma((chunks,)), dma, dma((chunks,)),
    ]
    return pl.pallas_call(
        kernel,
        out_shape=(pltpu.VMEM(hidden_state.shape, BF), pltpu.VMEM(cell_state.shape, F32)),
        in_specs=[any_space] * 9,
        out_specs=[pl.BlockSpec(memory_space=pltpu.VMEM)] * 2,
        scratch_shapes=scratch,
        compiler_params=pltpu.CompilerParams(vmem_limit_bytes=56 * 2**20, collective_id=1, has_side_effects=True),
        name="fused",
    )(frames, hidden_state, cell_state, w_gates, gate_bias[None], w_qkv, w_out, w_up, w_down)


def solution(mesh):
    spec = P("gy", "gx", None)
    return jax.shard_map(
        body,
        mesh=mesh,
        in_specs=(spec, spec, spec, P(), P(), P(), P(), P(), P()),
        out_specs=(spec, spec),
        check_vma=False,
    )
```

```python
import jax
import jax.numpy as jnp
from jax import lax
from jax.experimental import pallas as pl
from jax.experimental.pallas import tpu as pltpu
from jax.sharding import PartitionSpec as P

HEADS = 8
HDIM = 32
GRID = 8
SEG = 16
PITCH = 72
SIDE = 4
MESH = pl.DeviceIdType.MESH
BF = jnp.bfloat16
F32 = jnp.float32


def sigmoid(t):
    return 0.5 * jnp.tanh(0.5 * t) + 0.5


def layer_norm(values):
    center = values - jnp.mean(values, axis=-1, keepdims=True)
    spread = jnp.mean(center * center, axis=-1, keepdims=True)
    return center * lax.rsqrt(spread + 1e-05)


def shifted_row(a_ref, row, cells, lane):
    count, width = cells.shape
    wide = cells.astype(F32)
    a_ref[row, :, lane : lane + width] = pltpu.roll(wide, 1, 0).astype(BF)
    a_ref[row, :, lane + width : lane + 2 * width] = cells
    a_ref[row, :, lane + 2 * width : lane + 3 * width] = pltpu.roll(wide, count - 1, 0).astype(BF)


def patch_row(a_ref, row, left, right, lane):
    cols, width = a_ref.shape[1], left.shape[1]
    pos = lax.broadcasted_iota(jnp.int32, (SEG, width), 0)
    tile = a_ref[row, 0:SEG, lane : lane + width].astype(F32)
    a_ref[row, 0:SEG, lane : lane + width] = jnp.where(pos == 0, left, tile).astype(BF)
    lane += 2 * width
    tile = a_ref[row, cols - SEG : cols, lane : lane + width].astype(F32)
    a_ref[row, cols - SEG : cols, lane : lane + width] = jnp.where(pos == SEG - 1, right, tile).astype(BF)


def tap_rows(frame_taps, hidden_taps):
    return [v.reshape(-1, v.shape[-1]) for v in (frame_taps, hidden_taps)]


def mixed_taps(w_ref, mix_ref):
    cols, depth = w_ref.shape[1:3]
    step = 32

    def some(i, _):
        at = pl.ds(pl.multiple_of(i * step, step), step)
        for b in range(cols):
            ends = w_ref[0, b, at].astype(F32) + w_ref[2, b, at].astype(F32)
            middle = w_ref[1, b, at].astype(F32)
            mix_ref[0, b, at] = (0.5 * (ends + middle)).astype(BF)
            mix_ref[1, b, at] = (0.5 * (ends - middle)).astype(BF)
        return 0

    lax.fori_loop(0, depth // step, some, 0)


def conv_rows(a_ref, held, weights, row, rows, col, cols, low, high):
    x = [a_ref[row + i, col : col + cols, low:high] for i in range(rows + 2)]
    pairs = range(0, rows, 2)
    inputs = (
        [x[p] - x[p + 2] for p in pairs],
        [x[p + 1] + x[p + 2] for p in pairs],
        [x[p + 2] - x[p + 1] for p in pairs],
        [x[p + 1] - x[p + 3] for p in pairs],
    )
    m = [
        jnp.dot(jnp.concatenate(d, axis=0), g, preferred_element_type=F32) for d, g in zip(inputs, weights, strict=True)
    ]
    held[0], held[1] = m[1], m[2]
    even, odd = (held[0] + held[1]) + m[0], (held[0] - held[1]) - m[3]
    out = []
    for i in range(rows // 2):
        out += [even[i * cols : (i + 1) * cols], odd[i * cols : (i + 1) * cols]]
    return jnp.concatenate(out, axis=0)


def lstm(gates, cell):
    width = cell.shape[1]
    new_cell = sigmoid(gates[:, width : 2 * width]) * cell + sigmoid(gates[:, :width]) * jnp.tanh(
        gates[:, 2 * width : 3 * width]
    )
    return new_cell, sigmoid(gates[:, 3 * width :]) * jnp.tanh(new_cell)


def far_first(steps):
    return sorted(steps, key=lambda d: (-sum(min(v, SIDE - v) for v in d), sum(d) % 3, d))


class Torus:
    def __init__(self):
        gy, gx = lax.axis_index("gy"), lax.axis_index("gx")
        self.here = {"gy": gy, "gx": gx}
        self.parity = gy % 2
        k = gy // 2
        low, high, x, y = k // SIDE, gx % 2, gx // 2, k % SIDE
        self.low = low
        self.xs = [(x + d) % SIDE * 2 for d in range(SIDE)]
        self.ys = [(y + d) % SIDE for d in range(SIDE)]
        z = high * 2 + low
        self.zs = [((z + d) % SIDE % 2 * SIDE, (z + d) % SIDE // 2) for d in range(SIDE)]
        self.highs = [high, (high + 1) % 2]
        self.me = k * 2 * SIDE + gx

    def at(self, k, gx):
        return k * 2 * SIDE + gx, {"gy": 2 * k + self.parity, "gx": gx}

    def others(self):
        steps = [(a, b, c) for a in range(SIDE) for b in range(SIDE) for c in range(SIDE) if a or b or c]
        for a, b, c in far_first(steps):
            yield self.at(self.zs[c][0] + self.ys[b], self.xs[a] + self.zs[c][1])

    def half(self, low):
        steps = [(a, b, 2 * c) for a in range(SIDE) for b in range(SIDE) for c in range(2) if a or b or c]
        for a, b, c in far_first(steps):
            yield self.at(low * SIDE + self.ys[b], self.xs[a] + self.highs[c // 2])

    def mine(self, low):
        return self.at(low * SIDE + self.ys[0], self.xs[0] + self.highs[0])


class Shift:
    def __init__(self, src, dst, dy, dx, send_sem, recv_sem):
        gy, gx = lax.axis_index("gy"), lax.axis_index("gx")
        ny, nx = lax.axis_size("gy"), lax.axis_size("gx")

        def inside(y, x):
            return jnp.logical_and(jnp.logical_and(y >= 0, y < ny), jnp.logical_and(x >= 0, x < nx))

        self.dst = dst
        self.to = inside(gy + dy, gx + dx)
        self.come = inside(gy - dy, gx - dx)
        self.copy = pltpu.make_async_remote_copy(
            src_ref=src,
            dst_ref=dst,
            send_sem=send_sem,
            recv_sem=recv_sem,
            device_id={"gy": gy + dy, "gx": gx + dx},
            device_id_type=MESH,
        )

    def clear(self):
        @pl.when(jnp.logical_not(self.come))
        def _():
            self.dst[...] = jnp.zeros(self.dst.shape, self.dst.dtype)

    def start(self):
        @pl.when(self.to)
        def _():
            self.copy.start()

    def wait_recv(self):
        @pl.when(self.come)
        def _():
            self.copy.wait_recv()

    def wait_send(self):
        @pl.when(self.to)
        def _():
            self.copy.wait_send()


def shifts(pieces, cols_out, cols_in, corners_out, corners_in, send_sems, recv_sems):
    plan = []

    def add(src, dst, dy, dx):
        at = len(plan)
        plan.append(Shift(src, dst, dy, dx, send_sems.at[at], recv_sems.at[at]))

    for side, dx in ((1, -1), (0, 1)):
        add(cols_out.at[1 - side], cols_in.at[side], 0, dx)
    for dy, low in ((-1, 2), (1, 0)):
        for dx, side in ((-1, 1), (1, 0)):
            add(corners_out.at[3 - low - side], corners_in.at[low + side], dy, dx)
    for cells, rows_in in pieces:
        rows = cells.shape[0]
        add(cells.at[0], rows_in.at[1], -1, 0)
        add(cells.at[rows - 1], rows_in.at[0], 1, 0)
    return plan


def edge_columns(cells, cols_out, scratch, lane):
    rows, cols, width = cells.shape

    def eight(i, _):
        base = pl.multiple_of(i * 8, 8)
        low = [cells[base + k, 0:SEG, :].astype(F32)[0:1] for k in range(8)]
        high = [cells[base + k, cols - SEG : cols, :].astype(F32)[SEG - 1 : SEG] for k in range(8)]
        scratch[0, pl.ds(base, 8), lane : lane + width] = jnp.concatenate(low, axis=0)
        scratch[1, pl.ds(base, 8), lane : lane + width] = jnp.concatenate(high, axis=0)
        return 0

    lax.fori_loop(0, rows // 8, eight, 0)
    cols_out[:, :, lane : lane + width] = scratch[:, 0:rows, lane : lane + width].astype(BF)


def edge_corners(cells, corners_out, lane):
    rows, cols, width = cells.shape
    for k in range(4):
        row = (k // 2) * (rows - 1)
        if k % 2:
            cell = cells[row, cols - SEG : cols, :].astype(F32)[SEG - 1 : SEG]
        else:
            cell = cells[row, 0:SEG, :].astype(F32)[0:1]
        corners_out[k, :, lane : lane + width] = cell


def head_mask():
    row = lax.broadcasted_iota(jnp.int32, (256, 256), 0)
    col = lax.broadcasted_iota(jnp.int32, (256, 256), 1)
    heads = ((col % 128) // HDIM == row // 64).astype(F32).astype(BF)
    blocks = (col // 64 == row // 64).astype(F32).astype(BF)
    return heads, blocks


def attend_chunk(tokens, w_qkv, w_out, heads, blocks, wide, qkv, prob, outs):
    members = tokens.shape[0]
    cells = members * SEG
    wide[0:cells, :] = tokens.reshape(cells, 128).astype(F32)
    grouped = jnp.concatenate([wide[pl.ds(g, members, stride=SEG), :] for g in range(SEG)], axis=0).astype(BF)
    qkv[...] = jnp.dot(grouped, w_qkv[...], preferred_element_type=F32).astype(BF)
    zero = jnp.zeros((64, 128), BF)

    def spread(base, lane):
        pair = jnp.concatenate([qkv[base : base + 64, lane : lane + 128], qkv[base + 64 : base + 128, lane : lane + 128]], axis=1)
        return jnp.concatenate([pair] * 4, axis=0) * heads

    for base in range(0, cells, 128):
        for half in range(2):
            lane = half * 128
            q1 = jnp.concatenate([qkv[base : base + 64, lane : lane + 128], zero], axis=1)
            q2 = jnp.concatenate([zero, qkv[base + 64 : base + 128, lane : lane + 128]], axis=1)
            s = lax.dot_general(
                jnp.concatenate([q1, q2], axis=0),
                spread(base, 256 + lane),
                (((1,), (1,)), ((), ())),
                preferred_element_type=F32,
            )
            prob[half, base : base + 128, :] = jnp.minimum(jnp.exp(s * HDIM**-0.5), 3.3895e38).astype(BF)
    step = 512
    for base in range(0, cells, step):
        for half in range(2):
            raised = prob[half, base : base + step, :]
            total = jnp.dot(raised, blocks, preferred_element_type=F32)
            prob[half, base : base + step, :] = (raised.astype(F32) * (1.0 / total)).astype(BF)
    for base in range(0, cells, 128):
        for half in range(2):
            lane = half * 128
            o = jnp.dot(prob[half, base : base + 128, :], spread(base, 512 + lane), preferred_element_type=F32)
            outs[base : base + 64, lane : lane + 128] = o[:64, :128].astype(BF)
            outs[base + 64 : base + 128, lane : lane + 128] = o[64:, 128:].astype(BF)
    done = jnp.dot(outs[...], w_out[...], preferred_element_type=F32)
    for g in range(SEG):
        wide[g * PITCH : g * PITCH + members, :] = done[g * members : (g + 1) * members]


def mlp_rows(hidden, attended, w_up, w_down):
    mixed = hidden.astype(F32) + attended.astype(F32)
    normed = layer_norm(mixed).astype(BF)
    u = jnp.dot(normed, w_up[...], preferred_element_type=F32)
    twice = u + u * jnp.tanh(u * (0.7978845608 + 0.7978845608 * 0.044715 * (u * u)))
    return (mixed + 0.5 * jnp.dot(twice.astype(BF), w_down[...], preferred_element_type=F32)).astype(BF)


def kernel(*refs):
    names = iter(refs)
    take = lambda n: [next(names) for _ in range(n)]
    frames, hidden, cell, w_gates, bias_in, wqkv_in, wout_in, wup_in, wdown_in = take(9)
    outb, cl, last_hidden, last_landed, w_up, w_down = take(6)
    f1, f2, hd, w_f, w_h, mix_f, mix_h, bias_v, w_qkv, w_out = take(10)
    a1, a2, h1, h2, normed, tok, ret, land = take(8)
    rows_a, rows_h, cols_out, cols_in, corn_out, corn_in, edge = take(7)
    rows_b, cols_out_b, cols_in_b, corn_out_b, corn_in_b, edge_b = take(6)
    rows_1, cols_out_1, cols_in_1, corn_out_1, corn_in_1, edge_1 = take(6)
    part, held, wide, qkv, prob, outs = take(6)
    load_sem, send_a, recv_a, send_b, recv_b, send_1, recv_1, to_send, to_recv, back_send, back_recv = take(11)

    rows, cols, width = hd.shape
    latent = f1.shape[2]
    torus = Torus()
    gy, gx = torus.here["gy"], torus.here["gx"]
    ny, nx = lax.axis_size("gy"), lax.axis_size("gx")
    count = ny // 2 * nx
    me = torus.me
    split = 3 * latent
    step = 8
    groups = rows // step

    used = iter(range(64))

    def load(src, dst):
        return pltpu.make_async_copy(src, dst, load_sem.at[next(used)])

    first_loads = []
    bunch = 2 * step
    for row in range(0, rows, bunch):
        at = pl.ds(row, bunch)
        first_loads.append((load(frames.at[at, :, pl.ds(0, latent)], f1.at[at]), load(hidden.at[at], hd.at[at])))
    gate_loads = [
        load(w_gates.at[:, :, pl.ds(0, latent)], w_f),
        load(w_gates.at[:, :, pl.ds(latent, width)], w_h),
        load(cell, cl),
        load(bias_in, bias_v),
    ]
    load_f2 = load(frames.at[:, :, pl.ds(latent, latent)], f2)
    late_loads = [load(wqkv_in, w_qkv), load(wout_in, w_out), load(wup_in, w_up), load(wdown_in, w_down)]

    halo_a = shifts(((f1, rows_a), (hd, rows_h)), cols_out, cols_in, corn_out, corn_in, send_a, recv_a)
    halo_b = shifts(((f2, rows_b),), cols_out_b, cols_in_b, corn_out_b, corn_in_b, send_b, recv_b)
    halo_1 = shifts(((h1, rows_1),), cols_out_1, cols_in_1, corn_out_1, corn_in_1, send_1, recv_1)

    for pair in first_loads:
        for copy in pair:
            copy.start()
    barrier = pltpu.get_barrier_semaphore()

    for _, device in torus.others():
        pl.semaphore_signal(barrier, inc=1, device_id=device, device_id_type=MESH)
    greeted = count - 1
    for dy in (-1, 1):
        for dx in (-1, 0, 1):
            y, x = gy + dy, gx + dx
            near = jnp.logical_and(jnp.logical_and(y >= 0, y < ny), jnp.logical_and(x >= 0, x < nx))

            @pl.when(near)
            def _():
                pl.semaphore_signal(barrier, inc=1, device_id={"gy": y, "gx": x}, device_id_type=MESH)

            greeted = greeted + near.astype(jnp.int32)
    for copy in gate_loads + [load_f2] + late_loads:
        copy.start()
    for shift in halo_a + halo_b + halo_1:
        shift.clear()

    for g, pair in enumerate(first_loads):
        for copy in pair:
            copy.wait()

        def build(r, _):
            shifted_row(a1, r + 1, f1[r], 0)
            shifted_row(a1, r + 1, hd[r], split)
            return 0

        lax.fori_loop(g * bunch, g * bunch + bunch, build, 0, unroll=2)
    edge_columns(f1, cols_out, edge, 0)
    edge_columns(hd, cols_out, edge, latent)
    edge_corners(f1, corn_out, 0)
    edge_corners(hd, corn_out, latent)
    pl.semaphore_wait(barrier, greeted)
    for shift in halo_a:
        shift.start()
    for copy in gate_loads:
        copy.wait()
    bias = bias_v[...]
    mixed_taps(w_f, mix_f)
    mixed_taps(w_h, mix_h)

    def frame_taps():
        return [tap_rows(f, h)[0] for f, h in four()]

    def hidden_taps():
        return [tap_rows(f, h)[1] for f, h in four()]

    def four():
        return [(w_f[0], w_h[0]), (mix_f[0], mix_h[0]), (mix_f[1], mix_h[1]), (w_f[2], w_h[2])]

    def both_taps():
        return [jnp.concatenate(tap_rows(f, h), axis=0) for f, h in four()]

    def gates_of(a_ref, row, rows, col, cols):
        return conv_rows(a_ref, held, both_taps(), row, rows, col, cols, 0, a_ref.shape[2]) + bias

    def step_one(row, count_r, col, count_c):
        cells = count_r * count_c
        old = cl[pl.ds(row, count_r), col : col + count_c, :].reshape(cells, width)
        new_cell, hid = lstm(gates_of(a1, row, count_r, col, count_c), old)
        cl[pl.ds(row, count_r), col : col + count_c, :] = new_cell.reshape(count_r, count_c, width)
        h1[pl.ds(row, count_r), col : col + count_c, :] = hid.astype(BF).reshape(count_r, count_c, width)

    step_one(8, 16, SEG, cols - 2 * SEG)
    load_f2.wait()
    edge_columns(f2, cols_out_b, edge_b, 0)
    edge_corners(f2, corn_out_b, 0)
    for shift in halo_b:
        shift.start()
    step_one(24, 16, SEG, cols - 2 * SEG)

    def build_two(r, _):
        shifted_row(a2, r + 1, f2[r], 0)
        return 0

    lax.fori_loop(0, rows, build_two, 0, unroll=2)

    def patch(a_ref, side_in, parts):
        def eight(i, _):
            base = pl.multiple_of(i * 8, 8)
            left, right = side_in[0, pl.ds(base, 8), :], side_in[1, pl.ds(base, 8), :]
            for k in range(8):
                for low, high, lane in parts:
                    patch_row(a_ref, base + k + 1, left[k : k + 1, low:high], right[k : k + 1, low:high], lane)
            return 0

        lax.fori_loop(0, rows // 8, eight, 0)

    def outer(a_ref, rows_in, corners, low, lane):
        high = low + rows_in.shape[2]
        for end, row in ((0, 0), (1, rows + 1)):
            shifted_row(a_ref, row, rows_in[end], lane)
            patch_row(a_ref, row, corners[2 * end, :, low:high], corners[2 * end + 1, :, low:high], lane)

    for shift in halo_a:
        shift.wait_recv()
    edge[...] = cols_in[...].astype(F32)
    patch(a1, edge, ((0, latent, 0), (latent, latent + width, split)))
    outer(a1, rows_a, corn_in, 0, 0)
    outer(a1, rows_h, corn_in, latent, split)

    step_one(0, 8, 0, cols)
    step_one(rows - 8, 8, 0, cols)
    step_one(8, 32, 0, SEG)
    step_one(8, 32, cols - SEG, SEG)
    edge_columns(h1, cols_out_1, edge_1, 0)
    edge_corners(h1, corn_out_1, 0)
    for shift in halo_1:
        shift.start()
    for shift in halo_b:
        shift.wait_recv()
    edge_b[...] = cols_in_b[...].astype(F32)
    patch(a2, edge_b, ((0, latent, 0),))
    outer(a2, rows_b, corn_in_b, 0, 0)

    def build_three(r, _):
        shifted_row(a2, r + 1, h1[r], split)
        return 0

    lax.fori_loop(0, rows, build_three, 0, unroll=2)
    early = part.shape[0]
    for s in range(early):
        part[s] = conv_rows(a2, held, frame_taps(), s * step, step, 0, cols, 0, split) + bias
    for shift in halo_1:
        shift.wait_recv()
    edge_1[...] = cols_in_1[...].astype(F32)
    patch(a2, edge_1, ((0, width, split),))
    outer(a2, rows_1, corn_in_1, 0, split)

    quarters = cols // SEG
    sent = step * quarters

    def forward(c, j, device):
        return pltpu.make_async_remote_copy(
            src_ref=normed.at[c * count + j],
            dst_ref=tok.at[c, me],
            send_sem=to_send,
            recv_sem=to_recv.at[c],
            device_id=device,
            device_id_type=MESH,
        )

    def send_forward(s):
        c, low = s * sent // count, s * sent % count // sent
        for j, device in torus.half(low):
            forward(c, j, device).start()

    def send_last(s):
        c, low = s * sent // count, s * sent % count // sent

        @pl.when(torus.low != low)
        def _():
            forward(c, *torus.mine(low)).start()

    def step_two(s):
        row = s * step
        cells = step * cols
        if s < early:
            gates = part[s] + conv_rows(a2, held, hidden_taps(), row, step, 0, cols, split, a2.shape[2])
        else:
            gates = gates_of(a2, row, step, 0, cols)
        new_cell, hid = lstm(gates, cl[pl.ds(row, step)].reshape(cells, width))
        cl[pl.ds(row, step)] = new_cell.reshape(step, cols, width)
        hid = hid.astype(BF)
        h2[pl.ds(row * quarters, sent)] = hid.reshape(sent, SEG, width)
        normed[pl.ds(row * quarters, sent)] = layer_norm(hid.astype(F32)).astype(BF).reshape(sent, SEG, width)

    for s in range(groups):
        if s:
            send_last(s - 1)
            send_forward(s - 1)
        step_two(s)
    for copy in late_loads:
        copy.wait()
    heads, blocks = head_mask()
    chunks = tok.shape[0]

    def wait_for(ref, sem):
        pltpu.make_async_remote_copy(
            src_ref=ref, dst_ref=ref, send_sem=to_send, recv_sem=sem, device_id=torus.here, device_id_type=MESH
        ).wait_recv()

    def send_back(c):
        for m, device in torus.others():
            pltpu.make_async_remote_copy(
                src_ref=ret.at[c, m],
                dst_ref=land.at[c * count + me],
                send_sem=back_send,
                recv_sem=back_recv.at[c],
                device_id=device,
                device_id_type=MESH,
            ).start()

    for c in range(chunks):
        tok[c, me] = normed[c * count + me]
        if c == 0:
            send_last(groups - 1)
        wait_for(tok.at[c, pl.ds(0, count - 1)], to_recv.at[c])
        if c == 0:
            send_forward(groups - 1)
        else:
            send_back(c - 1)
        attend_chunk(tok[c], w_qkv, w_out, heads, blocks, wide, qkv, prob, outs)
        for m in range(count):
            ret[c, m] = wide[pl.ds(m, SEG, stride=PITCH), :].astype(BF)
        land[c * count + me] = ret[c, me]
    send_back(chunks - 1)
    for c in range(chunks):
        base = c * count
        wait_for(land.at[pl.ds(base, count - 1)], back_recv.at[c])
        if c == chunks - 1:
            last_hidden[...] = h2[pl.ds(base, count)]
            last_landed[...] = land[pl.ds(base, count)]
            break
        cells = count * SEG
        result = mlp_rows(
            h2[pl.ds(base, count)].reshape(cells, width), land[pl.ds(base, count)].reshape(cells, width), w_up, w_down
        )
        outb[pl.ds(c * SEG, SEG)] = result.reshape(SEG, cols, width)
    for shift in halo_a + halo_b + halo_1:
        shift.wait_send()
    for sem, source in ((to_send, tok), (back_send, ret)):
        most = source.at[:, pl.ds(0, count - 1)]
        pltpu.make_async_remote_copy(
            src_ref=most, dst_ref=most, send_sem=sem, recv_sem=to_recv.at[0],
            device_id=torus.here, device_id_type=MESH,
        ).wait_send()


def vmem(count):
    return [pl.BlockSpec(memory_space=pltpu.VMEM)] * count


def finish(block_in, cell_in, hidden, landed, w_up, w_down, block_out, cell_out, last, sems):
    done, cols, width = block_in.shape
    copies = [
        pltpu.make_async_copy(cell_in, cell_out, sems.at[0]),
        pltpu.make_async_copy(block_in, block_out.at[pl.ds(0, done)], sems.at[1]),
    ]
    for copy in copies:
        copy.start()
    rows = last.shape[0] // 2
    segs = hidden.shape[0] // 2
    for i in range(2):
        at = pl.ds(i * segs, segs)
        result = mlp_rows(hidden[at].reshape(-1, width), landed[at].reshape(-1, width), w_up, w_down)
        last[pl.ds(i * rows, rows)] = result.reshape(rows, cols, width)
        copy = pltpu.make_async_copy(
            last.at[pl.ds(i * rows, rows)], block_out.at[pl.ds(done + i * rows, rows)], sems.at[2 + i]
        )
        copy.start()
        copies.append(copy)
    for copy in copies:
        copy.wait()


def body(frames, hidden_state, cell_state, w_gates, gate_bias, w_qkv, w_out, w_up, w_down):
    rows, cols, width = hidden_state.shape
    latent = frames.shape[2] // 2
    gates = w_gates.shape[3]
    depth = 3 * (latent + width)
    members = lax.axis_size("gy") // 2 * lax.axis_size("gx")
    chunks = rows * cols // (members * SEG)
    cells = members * SEG
    any_space = pl.BlockSpec(memory_space=pl.ANY)
    dma = pltpu.SemaphoreType.DMA

    def vm(*shape, dtype=BF):
        return pltpu.VMEM(shape, dtype)

    def sides(span):
        return [
            vm(2, rows, span), vm(2, rows, span), vm(4, 1, span, dtype=F32), vm(4, 1, span, dtype=F32),
            vm(2, rows, span, dtype=F32),
        ]

    scratch = [
        vm(rows, cols, latent), vm(rows, cols, latent), vm(rows, cols, width),
        vm(3, 3, latent, gates), vm(3, 3, width, gates), vm(2, 3, latent, gates), vm(2, 3, width, gates),
        vm(1, gates, dtype=F32), vm(*w_qkv.shape), vm(*w_out.shape),
        vm(rows + 2, cols, depth), vm(rows + 2, cols, depth), vm(rows, cols, width),
        vm(chunks * members, SEG, width), vm(chunks * members, SEG, width),
        vm(chunks, members, SEG, width), vm(chunks, members, SEG, width),
        vm(chunks * members, SEG, width),
        vm(2, cols, latent), vm(2, cols, width), *sides(latent + width),
        vm(2, cols, latent), *sides(latent),
        vm(2, cols, width), *sides(width),
        vm(3, 8 * cols, gates, dtype=F32), vm(2, 4 * cols, gates, dtype=F32),
        vm(SEG * PITCH, width, dtype=F32), vm(cells, 3 * HEADS * HDIM), vm(2, cells, 256), vm(cells, HEADS * HDIM),
        dma((64,)), dma((10,)), dma((10,)), dma((8,)), dma((8,)), dma((8,)), dma((8,)),
        dma, dma((chunks,)), dma, dma((chunks,)),
    ]
    early = pl.pallas_call(
        kernel,
        out_shape=(
            pltpu.VMEM((rows - SEG, cols, width), BF),
            pltpu.VMEM(cell_state.shape, F32),
            pltpu.VMEM((members, SEG, width), BF),
            pltpu.VMEM((members, SEG, width), BF),
            pltpu.VMEM(w_up.shape, BF),
            pltpu.VMEM(w_down.shape, BF),
        ),
        in_specs=[any_space] * 9,
        out_specs=vmem(6),
        scratch_shapes=scratch,
        compiler_params=pltpu.CompilerParams(vmem_limit_bytes=56 * 2**20, collective_id=1, has_side_effects=True),
        name="fused",
    )(frames, hidden_state, cell_state, w_gates, gate_bias[None], w_qkv, w_out, w_up, w_down)
    return pl.pallas_call(
        finish,
        out_shape=(jax.ShapeDtypeStruct(hidden_state.shape, BF), jax.ShapeDtypeStruct(cell_state.shape, F32)),
        in_specs=vmem(6),
        out_specs=[any_space] * 2,
        scratch_shapes=[vm(SEG, cols, width), dma((4,))],
        compiler_params=pltpu.CompilerParams(vmem_limit_bytes=16 * 2**20),
        name="finish",
    )(*early)


def solution(mesh):
    spec = P("gy", "gx", None)
    return jax.shard_map(
        body,
        mesh=mesh,
        in_specs=(spec, spec, spec, P(), P(), P(), P(), P(), P()),
        out_specs=(spec, spec),
        check_vma=False,
    )
```

```python
import jax
import jax.numpy as jnp
from jax import lax
from jax.experimental import pallas as pl
from jax.experimental.pallas import tpu as pltpu
from jax.sharding import PartitionSpec as P

HEADS = 8
HDIM = 32
GRID = 8
SEG = 16
PITCH = 72
SIDE = 4
MESH = pl.DeviceIdType.MESH
BF = jnp.bfloat16
F32 = jnp.float32


def sigmoid(t):
    return 0.5 * jnp.tanh(0.5 * t) + 0.5


def layer_norm(values):
    center = values - jnp.mean(values, axis=-1, keepdims=True)
    spread = jnp.mean(center * center, axis=-1, keepdims=True)
    return center * lax.rsqrt(spread + 1e-05)


def shifted_row(a_ref, row, cells, lane):
    count, width = cells.shape
    wide = cells.astype(F32)
    a_ref[row, :, lane : lane + width] = pltpu.roll(wide, 1, 0).astype(BF)
    a_ref[row, :, lane + width : lane + 2 * width] = cells
    a_ref[row, :, lane + 2 * width : lane + 3 * width] = pltpu.roll(wide, count - 1, 0).astype(BF)


def patch_row(a_ref, row, left, right, lane):
    cols, width = a_ref.shape[1], left.shape[1]
    pos = lax.broadcasted_iota(jnp.int32, (SEG, width), 0)
    tile = a_ref[row, 0:SEG, lane : lane + width].astype(F32)
    a_ref[row, 0:SEG, lane : lane + width] = jnp.where(pos == 0, left, tile).astype(BF)
    lane += 2 * width
    tile = a_ref[row, cols - SEG : cols, lane : lane + width].astype(F32)
    a_ref[row, cols - SEG : cols, lane : lane + width] = jnp.where(pos == SEG - 1, right, tile).astype(BF)


def tap_rows(frame_taps, hidden_taps):
    return [v.reshape(-1, v.shape[-1]) for v in (frame_taps, hidden_taps)]


def mixed_taps(w_ref, mix_ref):
    cols, depth = w_ref.shape[1:3]
    step = 32

    def some(i, _):
        at = pl.ds(pl.multiple_of(i * step, step), step)
        for b in range(cols):
            ends = w_ref[0, b, at].astype(F32) + w_ref[2, b, at].astype(F32)
            middle = w_ref[1, b, at].astype(F32)
            mix_ref[0, b, at] = (0.5 * (ends + middle)).astype(BF)
            mix_ref[1, b, at] = (0.5 * (ends - middle)).astype(BF)
        return 0

    lax.fori_loop(0, depth // step, some, 0)


def conv_rows(a_ref, held, weights, row, rows, col, cols, low, high):
    x = [a_ref[row + i, col : col + cols, low:high] for i in range(rows + 2)]
    pairs = range(0, rows, 2)
    inputs = (
        [x[p] - x[p + 2] for p in pairs],
        [x[p + 1] + x[p + 2] for p in pairs],
        [x[p + 2] - x[p + 1] for p in pairs],
        [x[p + 1] - x[p + 3] for p in pairs],
    )
    m = [
        jnp.dot(jnp.concatenate(d, axis=0), g, preferred_element_type=F32) for d, g in zip(inputs, weights, strict=True)
    ]
    held[0], held[1] = m[1], m[2]
    even, odd = (held[0] + held[1]) + m[0], (held[0] - held[1]) - m[3]
    out = []
    for i in range(rows // 2):
        out += [even[i * cols : (i + 1) * cols], odd[i * cols : (i + 1) * cols]]
    return jnp.concatenate(out, axis=0)


def lstm(gates, cell):
    width = cell.shape[1]
    new_cell = sigmoid(gates[:, width : 2 * width]) * cell + sigmoid(gates[:, :width]) * jnp.tanh(
        gates[:, 2 * width : 3 * width]
    )
    return new_cell, sigmoid(gates[:, 3 * width :]) * jnp.tanh(new_cell)


def far_first(steps):
    return sorted(steps, key=lambda d: (-sum(min(v, SIDE - v) for v in d), sum(d) % 3, d))


class Torus:
    def __init__(self):
        gy, gx = lax.axis_index("gy"), lax.axis_index("gx")
        self.here = {"gy": gy, "gx": gx}
        self.parity = gy % 2
        k = gy // 2
        low, high, x, y = k // SIDE, gx % 2, gx // 2, k % SIDE
        self.low = low
        self.xs = [(x + d) % SIDE * 2 for d in range(SIDE)]
        self.ys = [(y + d) % SIDE for d in range(SIDE)]
        z = high * 2 + low
        self.zs = [((z + d) % SIDE % 2 * SIDE, (z + d) % SIDE // 2) for d in range(SIDE)]
        self.highs = [high, (high + 1) % 2]
        self.me = k * 2 * SIDE + gx

    def at(self, k, gx):
        return k * 2 * SIDE + gx, {"gy": 2 * k + self.parity, "gx": gx}

    def others(self):
        steps = [(a, b, c) for a in range(SIDE) for b in range(SIDE) for c in range(SIDE) if a or b or c]
        for a, b, c in far_first(steps):
            yield self.at(self.zs[c][0] + self.ys[b], self.xs[a] + self.zs[c][1])

    def half(self, low):
        steps = [(a, b, 2 * c) for a in range(SIDE) for b in range(SIDE) for c in range(2) if a or b or c]
        for a, b, c in far_first(steps):
            yield self.at(low * SIDE + self.ys[b], self.xs[a] + self.highs[c // 2])

    def mine(self, low):
        return self.at(low * SIDE + self.ys[0], self.xs[0] + self.highs[0])


class Shift:
    def __init__(self, src, dst, dy, dx, send_sem, recv_sem):
        gy, gx = lax.axis_index("gy"), lax.axis_index("gx")
        ny, nx = lax.axis_size("gy"), lax.axis_size("gx")

        def inside(y, x):
            return jnp.logical_and(jnp.logical_and(y >= 0, y < ny), jnp.logical_and(x >= 0, x < nx))

        self.dst = dst
        self.to = inside(gy + dy, gx + dx)
        self.come = inside(gy - dy, gx - dx)
        self.copy = pltpu.make_async_remote_copy(
            src_ref=src,
            dst_ref=dst,
            send_sem=send_sem,
            recv_sem=recv_sem,
            device_id={"gy": gy + dy, "gx": gx + dx},
            device_id_type=MESH,
        )

    def clear(self):
        @pl.when(jnp.logical_not(self.come))
        def _():
            self.dst[...] = jnp.zeros(self.dst.shape, self.dst.dtype)

    def start(self):
        @pl.when(self.to)
        def _():
            self.copy.start()

    def wait_recv(self):
        @pl.when(self.come)
        def _():
            self.copy.wait_recv()

    def wait_send(self):
        @pl.when(self.to)
        def _():
            self.copy.wait_send()


def shifts(pieces, cols_out, cols_in, corners_out, corners_in, send_sems, recv_sems):
    plan = []

    def add(src, dst, dy, dx):
        at = len(plan)
        plan.append(Shift(src, dst, dy, dx, send_sems.at[at], recv_sems.at[at]))

    for side, dx in ((1, -1), (0, 1)):
        add(cols_out.at[1 - side], cols_in.at[side], 0, dx)
    for dy, low in ((-1, 2), (1, 0)):
        for dx, side in ((-1, 1), (1, 0)):
            add(corners_out.at[3 - low - side], corners_in.at[low + side], dy, dx)
    for cells, rows_in in pieces:
        rows = cells.shape[0]
        add(cells.at[0], rows_in.at[1], -1, 0)
        add(cells.at[rows - 1], rows_in.at[0], 1, 0)
    return plan


def edge_columns(cells, cols_out, scratch, lane):
    rows, cols, width = cells.shape

    def eight(i, _):
        base = pl.multiple_of(i * 8, 8)
        low = [cells[base + k, 0:SEG, :].astype(F32)[0:1] for k in range(8)]
        high = [cells[base + k, cols - SEG : cols, :].astype(F32)[SEG - 1 : SEG] for k in range(8)]
        scratch[0, pl.ds(base, 8), lane : lane + width] = jnp.concatenate(low, axis=0)
        scratch[1, pl.ds(base, 8), lane : lane + width] = jnp.concatenate(high, axis=0)
        return 0

    lax.fori_loop(0, rows // 8, eight, 0)
    cols_out[:, :, lane : lane + width] = scratch[:, 0:rows, lane : lane + width].astype(BF)


def edge_corners(cells, corners_out, lane):
    rows, cols, width = cells.shape
    for k in range(4):
        row = (k // 2) * (rows - 1)
        if k % 2:
            cell = cells[row, cols - SEG : cols, :].astype(F32)[SEG - 1 : SEG]
        else:
            cell = cells[row, 0:SEG, :].astype(F32)[0:1]
        corners_out[k, :, lane : lane + width] = cell


def head_mask():
    row = lax.broadcasted_iota(jnp.int32, (256, 256), 0)
    col = lax.broadcasted_iota(jnp.int32, (256, 256), 1)
    heads = ((col % 128) // HDIM == row // 64).astype(F32).astype(BF)
    blocks = (col // 64 == row // 64).astype(F32).astype(BF)
    return heads, blocks


def attend_chunk(tokens, w_qkv, w_out, heads, blocks, wide, qkv, prob, outs):
    members = tokens.shape[0]
    cells = members * SEG
    wide[0:cells, :] = tokens.reshape(cells, 128).astype(F32)
    grouped = jnp.concatenate([wide[pl.ds(g, members, stride=SEG), :] for g in range(SEG)], axis=0).astype(BF)
    qkv[...] = jnp.dot(grouped, w_qkv[...], preferred_element_type=F32).astype(BF)
    zero = jnp.zeros((64, 128), BF)

    def spread(base, lane):
        pair = jnp.concatenate([qkv[base : base + 64, lane : lane + 128], qkv[base + 64 : base + 128, lane : lane + 128]], axis=1)
        return jnp.concatenate([pair] * 4, axis=0) * heads

    for base in range(0, cells, 128):
        for half in range(2):
            lane = half * 128
            q1 = jnp.concatenate([qkv[base : base + 64, lane : lane + 128], zero], axis=1)
            q2 = jnp.concatenate([zero, qkv[base + 64 : base + 128, lane : lane + 128]], axis=1)
            s = lax.dot_general(
                jnp.concatenate([q1, q2], axis=0),
                spread(base, 256 + lane),
                (((1,), (1,)), ((), ())),
                preferred_element_type=F32,
            )
            prob[half, base : base + 128, :] = jnp.minimum(jnp.exp(s * HDIM**-0.5), 3.3895e38).astype(BF)
    step = 512
    for base in range(0, cells, step):
        for half in range(2):
            raised = prob[half, base : base + step, :]
            total = jnp.dot(raised, blocks, preferred_element_type=F32)
            prob[half, base : base + step, :] = (raised.astype(F32) * (1.0 / total)).astype(BF)
    for base in range(0, cells, 128):
        for half in range(2):
            lane = half * 128
            o = jnp.dot(prob[half, base : base + 128, :], spread(base, 512 + lane), preferred_element_type=F32)
            outs[base : base + 64, lane : lane + 128] = o[:64, :128].astype(BF)
            outs[base + 64 : base + 128, lane : lane + 128] = o[64:, 128:].astype(BF)
    done = jnp.dot(outs[...], w_out[...], preferred_element_type=F32)
    for g in range(SEG):
        wide[g * PITCH : g * PITCH + members, :] = done[g * members : (g + 1) * members]


def mlp_rows(hidden, attended, w_up, w_down):
    mixed = hidden.astype(F32) + attended.astype(F32)
    normed = layer_norm(mixed).astype(BF)
    u = jnp.dot(normed, w_up[...], preferred_element_type=F32)
    twice = u + u * jnp.tanh(u * (0.7978845608 + 0.7978845608 * 0.044715 * (u * u)))
    return (mixed + 0.5 * jnp.dot(twice.astype(BF), w_down[...], preferred_element_type=F32)).astype(BF)


def kernel(*refs):
    names = iter(refs)
    take = lambda n: [next(names) for _ in range(n)]
    frames, hidden, cell, w_gates, bias_in, wqkv_in, wout_in, wup_in, wdown_in = take(9)
    outb, cl, last_hidden, last_landed, w_up, w_down = take(6)
    f1, f2, hd, w_f, w_h, mix_f, mix_h, bias_v, w_qkv, w_out = take(10)
    a1, a2, h1, h2, normed, tok, ret, land = take(8)
    rows_a, rows_h, cols_out, cols_in, corn_out, corn_in, edge = take(7)
    rows_b, cols_out_b, cols_in_b, corn_out_b, corn_in_b, edge_b = take(6)
    rows_1, cols_out_1, cols_in_1, corn_out_1, corn_in_1, edge_1 = take(6)
    part, held, wide, qkv, prob, outs = take(6)
    load_sem, send_a, recv_a, send_b, recv_b, send_1, recv_1, to_send, to_recv, back_send, back_recv = take(11)

    rows, cols, width = hd.shape
    latent = f1.shape[2]
    torus = Torus()
    gy, gx = torus.here["gy"], torus.here["gx"]
    ny, nx = lax.axis_size("gy"), lax.axis_size("gx")
    count = ny // 2 * nx
    me = torus.me
    split = 3 * latent
    step = 8
    groups = rows // step

    used = iter(range(64))

    def load(src, dst):
        return pltpu.make_async_copy(src, dst, load_sem.at[next(used)])

    first_loads = []
    bunch = 2 * step
    for row in range(0, rows, bunch):
        at = pl.ds(row, bunch)
        first_loads.append((load(frames.at[at, :, pl.ds(0, latent)], f1.at[at]), load(hidden.at[at], hd.at[at])))
    gate_loads = [
        load(w_gates.at[:, :, pl.ds(0, latent)], w_f),
        load(w_gates.at[:, :, pl.ds(latent, width)], w_h),
        load(cell, cl),
        load(bias_in, bias_v),
    ]
    load_f2 = load(frames.at[:, :, pl.ds(latent, latent)], f2)
    late_loads = [load(wqkv_in, w_qkv), load(wout_in, w_out), load(wup_in, w_up), load(wdown_in, w_down)]

    halo_a = shifts(((f1, rows_a), (hd, rows_h)), cols_out, cols_in, corn_out, corn_in, send_a, recv_a)
    halo_b = shifts(((f2, rows_b),), cols_out_b, cols_in_b, corn_out_b, corn_in_b, send_b, recv_b)
    halo_1 = shifts(((h1, rows_1),), cols_out_1, cols_in_1, corn_out_1, corn_in_1, send_1, recv_1)

    for pair in first_loads:
        for copy in pair:
            copy.start()
    barrier = pltpu.get_barrier_semaphore()

    for _, device in torus.others():
        pl.semaphore_signal(barrier, inc=1, device_id=device, device_id_type=MESH)
    greeted = count - 1
    for dy in (-1, 1):
        for dx in (-1, 0, 1):
            y, x = gy + dy, gx + dx
            near = jnp.logical_and(jnp.logical_and(y >= 0, y < ny), jnp.logical_and(x >= 0, x < nx))

            @pl.when(near)
            def _():
                pl.semaphore_signal(barrier, inc=1, device_id={"gy": y, "gx": x}, device_id_type=MESH)

            greeted = greeted + near.astype(jnp.int32)
    for copy in gate_loads + [load_f2] + late_loads:
        copy.start()
    for shift in halo_a + halo_b + halo_1:
        shift.clear()

    for g, pair in enumerate(first_loads):
        for copy in pair:
            copy.wait()

        def build(r, _):
            shifted_row(a1, r + 1, f1[r], 0)
            shifted_row(a1, r + 1, hd[r], split)
            return 0

        lax.fori_loop(g * bunch, g * bunch + bunch, build, 0, unroll=2)
    edge_columns(f1, cols_out, edge, 0)
    edge_columns(hd, cols_out, edge, latent)
    edge_corners(f1, corn_out, 0)
    edge_corners(hd, corn_out, latent)
    for copy in gate_loads:
        copy.wait()
    bias = bias_v[...]
    mixed_taps(w_f, mix_f)
    mixed_taps(w_h, mix_h)
    load_f2.wait()
    edge_columns(f2, cols_out_b, edge_b, 0)
    edge_corners(f2, corn_out_b, 0)
    def build_two(r, _):
        shifted_row(a2, r + 1, f2[r], 0)
        return 0

    lax.fori_loop(0, rows, build_two, 0, unroll=2)
    pl.semaphore_wait(barrier, greeted)
    for shift in halo_a:
        shift.start()

    def frame_taps():
        return [tap_rows(f, h)[0] for f, h in four()]

    def hidden_taps():
        return [tap_rows(f, h)[1] for f, h in four()]

    def four():
        return [(w_f[0], w_h[0]), (mix_f[0], mix_h[0]), (mix_f[1], mix_h[1]), (w_f[2], w_h[2])]

    def both_taps():
        return [jnp.concatenate(tap_rows(f, h), axis=0) for f, h in four()]

    def gates_of(a_ref, row, rows, col, cols):
        return conv_rows(a_ref, held, both_taps(), row, rows, col, cols, 0, a_ref.shape[2]) + bias

    def step_one(row, count_r, col, count_c):
        cells = count_r * count_c
        old = cl[pl.ds(row, count_r), col : col + count_c, :].reshape(cells, width)
        new_cell, hid = lstm(gates_of(a1, row, count_r, col, count_c), old)
        cl[pl.ds(row, count_r), col : col + count_c, :] = new_cell.reshape(count_r, count_c, width)
        h1[pl.ds(row, count_r), col : col + count_c, :] = hid.astype(BF).reshape(count_r, count_c, width)

    step_one(8, 16, SEG, cols - 2 * SEG)
    for shift in halo_b:
        shift.start()
    step_one(24, 16, SEG, cols - 2 * SEG)


    def patch(a_ref, side_in, parts):
        def eight(i, _):
            base = pl.multiple_of(i * 8, 8)
            left, right = side_in[0, pl.ds(base, 8), :], side_in[1, pl.ds(base, 8), :]
            for k in range(8):
                for low, high, lane in parts:
                    patch_row(a_ref, base + k + 1, left[k : k + 1, low:high], right[k : k + 1, low:high], lane)
            return 0

        lax.fori_loop(0, rows // 8, eight, 0)

    def outer(a_ref, rows_in, corners, low, lane):
        high = low + rows_in.shape[2]
        for end, row in ((0, 0), (1, rows + 1)):
            shifted_row(a_ref, row, rows_in[end], lane)
            patch_row(a_ref, row, corners[2 * end, :, low:high], corners[2 * end + 1, :, low:high], lane)

    for shift in halo_a:
        shift.wait_recv()
    edge[...] = cols_in[...].astype(F32)
    patch(a1, edge, ((0, latent, 0), (latent, latent + width, split)))
    outer(a1, rows_a, corn_in, 0, 0)
    outer(a1, rows_h, corn_in, latent, split)

    step_one(0, 8, 0, cols)
    step_one(rows - 8, 8, 0, cols)
    step_one(8, 32, 0, SEG)
    step_one(8, 32, cols - SEG, SEG)
    edge_columns(h1, cols_out_1, edge_1, 0)
    edge_corners(h1, corn_out_1, 0)
    for shift in halo_1:
        shift.start()
    for shift in halo_b:
        shift.wait_recv()
    edge_b[...] = cols_in_b[...].astype(F32)
    patch(a2, edge_b, ((0, latent, 0),))
    outer(a2, rows_b, corn_in_b, 0, 0)

    def build_three(r, _):
        shifted_row(a2, r + 1, h1[r], split)
        return 0

    lax.fori_loop(0, rows, build_three, 0, unroll=2)
    early = part.shape[0]
    for s in range(early):
        part[s] = conv_rows(a2, held, frame_taps(), s * step, step, 0, cols, 0, split) + bias
    for shift in halo_1:
        shift.wait_recv()
    edge_1[...] = cols_in_1[...].astype(F32)
    patch(a2, edge_1, ((0, width, split),))
    outer(a2, rows_1, corn_in_1, 0, split)

    quarters = cols // SEG
    sent = step * quarters

    def forward(c, j, device):
        return pltpu.make_async_remote_copy(
            src_ref=normed.at[c * count + j],
            dst_ref=tok.at[c, me],
            send_sem=to_send,
            recv_sem=to_recv.at[c],
            device_id=device,
            device_id_type=MESH,
        )

    def send_forward(s):
        c, low = s * sent // count, s * sent % count // sent
        for j, device in torus.half(low):
            forward(c, j, device).start()

    def send_last(s):
        c, low = s * sent // count, s * sent % count // sent

        @pl.when(torus.low != low)
        def _():
            forward(c, *torus.mine(low)).start()

    def step_two(s):
        row = s * step
        cells = step * cols
        if s < early:
            gates = part[s] + conv_rows(a2, held, hidden_taps(), row, step, 0, cols, split, a2.shape[2])
        else:
            gates = gates_of(a2, row, step, 0, cols)
        new_cell, hid = lstm(gates, cl[pl.ds(row, step)].reshape(cells, width))
        cl[pl.ds(row, step)] = new_cell.reshape(step, cols, width)
        hid = hid.astype(BF)
        h2[pl.ds(row * quarters, sent)] = hid.reshape(sent, SEG, width)
        normed[pl.ds(row * quarters, sent)] = layer_norm(hid.astype(F32)).astype(BF).reshape(sent, SEG, width)

    for s in range(groups):
        if s:
            send_last(s - 1)
            send_forward(s - 1)
        step_two(s)
    for copy in late_loads:
        copy.wait()
    heads, blocks = head_mask()
    chunks = tok.shape[0]

    def wait_for(ref, sem):
        pltpu.make_async_remote_copy(
            src_ref=ref, dst_ref=ref, send_sem=to_send, recv_sem=sem, device_id=torus.here, device_id_type=MESH
        ).wait_recv()

    def send_back(c):
        for m, device in torus.others():
            pltpu.make_async_remote_copy(
                src_ref=ret.at[c, m],
                dst_ref=land.at[c * count + me],
                send_sem=back_send,
                recv_sem=back_recv.at[c],
                device_id=device,
                device_id_type=MESH,
            ).start()

    for c in range(chunks):
        tok[c, me] = normed[c * count + me]
        if c == 0:
            send_last(groups - 1)
        wait_for(tok.at[c, pl.ds(0, count - 1)], to_recv.at[c])
        if c == 0:
            send_forward(groups - 1)
        else:
            send_back(c - 1)
        attend_chunk(tok[c], w_qkv, w_out, heads, blocks, wide, qkv, prob, outs)
        for m in range(count):
            ret[c, m] = wide[pl.ds(m, SEG, stride=PITCH), :].astype(BF)
        land[c * count + me] = ret[c, me]
    send_back(chunks - 1)
    for c in range(chunks):
        base = c * count
        wait_for(land.at[pl.ds(base, count - 1)], back_recv.at[c])
        if c == chunks - 1:
            last_hidden[...] = h2[pl.ds(base, count)]
            last_landed[...] = land[pl.ds(base, count)]
            break
        cells = count * SEG
        result = mlp_rows(
            h2[pl.ds(base, count)].reshape(cells, width), land[pl.ds(base, count)].reshape(cells, width), w_up, w_down
        )
        outb[pl.ds(c * SEG, SEG)] = result.reshape(SEG, cols, width)
    for shift in halo_a + halo_b + halo_1:
        shift.wait_send()
    for sem, source in ((to_send, tok), (back_send, ret)):
        most = source.at[:, pl.ds(0, count - 1)]
        pltpu.make_async_remote_copy(
            src_ref=most, dst_ref=most, send_sem=sem, recv_sem=to_recv.at[0],
            device_id=torus.here, device_id_type=MESH,
        ).wait_send()


def vmem(count):
    return [pl.BlockSpec(memory_space=pltpu.VMEM)] * count


def finish(block_in, cell_in, hidden, landed, w_up, w_down, block_out, cell_out, last, sems):
    done, cols, width = block_in.shape
    copies = [
        pltpu.make_async_copy(cell_in, cell_out, sems.at[0]),
        pltpu.make_async_copy(block_in, block_out.at[pl.ds(0, done)], sems.at[1]),
    ]
    for copy in copies:
        copy.start()
    rows = last.shape[0] // 2
    segs = hidden.shape[0] // 2
    for i in range(2):
        at = pl.ds(i * segs, segs)
        result = mlp_rows(hidden[at].reshape(-1, width), landed[at].reshape(-1, width), w_up, w_down)
        last[pl.ds(i * rows, rows)] = result.reshape(rows, cols, width)
        copy = pltpu.make_async_copy(
            last.at[pl.ds(i * rows, rows)], block_out.at[pl.ds(done + i * rows, rows)], sems.at[2 + i]
        )
        copy.start()
        copies.append(copy)
    for copy in copies:
        copy.wait()


def body(frames, hidden_state, cell_state, w_gates, gate_bias, w_qkv, w_out, w_up, w_down):
    rows, cols, width = hidden_state.shape
    latent = frames.shape[2] // 2
    gates = w_gates.shape[3]
    depth = 3 * (latent + width)
    members = lax.axis_size("gy") // 2 * lax.axis_size("gx")
    chunks = rows * cols // (members * SEG)
    cells = members * SEG
    any_space = pl.BlockSpec(memory_space=pl.ANY)
    dma = pltpu.SemaphoreType.DMA

    def vm(*shape, dtype=BF):
        return pltpu.VMEM(shape, dtype)

    def sides(span):
        return [
            vm(2, rows, span), vm(2, rows, span), vm(4, 1, span, dtype=F32), vm(4, 1, span, dtype=F32),
            vm(2, rows, span, dtype=F32),
        ]

    scratch = [
        vm(rows, cols, latent), vm(rows, cols, latent), vm(rows, cols, width),
        vm(3, 3, latent, gates), vm(3, 3, width, gates), vm(2, 3, latent, gates), vm(2, 3, width, gates),
        vm(1, gates, dtype=F32), vm(*w_qkv.shape), vm(*w_out.shape),
        vm(rows + 2, cols, depth), vm(rows + 2, cols, depth), vm(rows, cols, width),
        vm(chunks * members, SEG, width), vm(chunks * members, SEG, width),
        vm(chunks, members, SEG, width), vm(chunks, members, SEG, width),
        vm(chunks * members, SEG, width),
        vm(2, cols, latent), vm(2, cols, width), *sides(latent + width),
        vm(2, cols, latent), *sides(latent),
        vm(2, cols, width), *sides(width),
        vm(3, 8 * cols, gates, dtype=F32), vm(2, 4 * cols, gates, dtype=F32),
        vm(SEG * PITCH, width, dtype=F32), vm(cells, 3 * HEADS * HDIM), vm(2, cells, 256), vm(cells, HEADS * HDIM),
        dma((64,)), dma((10,)), dma((10,)), dma((8,)), dma((8,)), dma((8,)), dma((8,)),
        dma, dma((chunks,)), dma, dma((chunks,)),
    ]
    early = pl.pallas_call(
        kernel,
        out_shape=(
            pltpu.VMEM((rows - SEG, cols, width), BF),
            pltpu.VMEM(cell_state.shape, F32),
            pltpu.VMEM((members, SEG, width), BF),
            pltpu.VMEM((members, SEG, width), BF),
            pltpu.VMEM(w_up.shape, BF),
            pltpu.VMEM(w_down.shape, BF),
        ),
        in_specs=[any_space] * 9,
        out_specs=vmem(6),
        scratch_shapes=scratch,
        compiler_params=pltpu.CompilerParams(vmem_limit_bytes=56 * 2**20, collective_id=1, has_side_effects=True),
        name="fused",
    )(frames, hidden_state, cell_state, w_gates, gate_bias[None], w_qkv, w_out, w_up, w_down)
    return pl.pallas_call(
        finish,
        out_shape=(jax.ShapeDtypeStruct(hidden_state.shape, BF), jax.ShapeDtypeStruct(cell_state.shape, F32)),
        in_specs=vmem(6),
        out_specs=[any_space] * 2,
        scratch_shapes=[vm(SEG, cols, width), dma((4,))],
        compiler_params=pltpu.CompilerParams(vmem_limit_bytes=16 * 2**20),
        name="finish",
    )(*early)


def solution(mesh):
    spec = P("gy", "gx", None)
    return jax.shard_map(
        body,
        mesh=mesh,
        in_specs=(spec, spec, spec, P(), P(), P(), P(), P(), P()),
        out_specs=(spec, spec),
        check_vma=False,
    )
```
